256 devices in a mesh: seq: 16 (over x_hi, y, core), tp: 16 (over x_lo, z).
Axes of the slice: x: 4 (x_hi: 2, x_lo: 2; x = x_hi * 2 + x_lo), y: 4, z: 8, core: 2. Of those that a mesh axis runs over, the one named last changes fastest.
Arguments:
- hidden: bfloat16 [4096, 4096], P('seq', 'tp'), may hold values from -6 to 6
- norm_gain: float32 [4096], replicated, may hold values from 0.25 to 1.75
- value_weight: bfloat16 [4096, 4096], P(None, 'tp'), may hold values from -0.09375 to 0.09375
- gate_weight: bfloat16 [4096, 4096], P(None, 'tp'), may hold values from -0.09375 to 0.09375
- value_taps: float32 [3, 4096], P(None, 'tp'), may hold values from -3 to 3
- gate_taps: float32 [3, 4096], P(None, 'tp'), may hold values from -3 to 3
- rates: float32 [16, 4096], P(None, 'tp'), may hold values from 1.2207031e-05 to 0.05, as said below
- residues: float32 [16, 4096], P(None, 'tp'), may hold values from -1.5 to 1.5
- out_weight: bfloat16 [4096, 4096], P('tp'), may hold values from -0.125 to 0.125
Outputs:
- mixed: bfloat16 [4096, 4096], P('seq', 'tp')
The draws below stay inside these ranges and needn't reach their ends.
Inputs may be any that keep to these rules, and one draw needn't show every extreme that they name: Decay rates are positive.
All inputs are finite; a program needn't handle non-finite values.
Results may differ from the reference program's by a relative error of at most 0.0076.
Values may be sent and summed in bfloat16 or wider, within the bound.
No kernel may reach another device: no remote copies, remote signals or barrier semaphores. Data moves between devices by JAX's collectives and lax.ppermute only.
A program may use at most 128 MiB of HBM per device.

```python
import math
import jax
import jax.numpy as jnp
from jax import lax

D = 4096
MODES = 16
LENGTH = 4096


def draw_rates(key, part):
    lowest = 0.05 / LENGTH
    highest = 0.05
    unit = jax.random.uniform(key, (MODES, D), jnp.float32)
    return jnp.exp(jnp.log(lowest) + unit * (jnp.log(highest) - jnp.log(lowest)))


def with_spikes(drawn, rng, source, target, parts, factor):
    def block_of(axis_at):
        return (jnp.arange(drawn.shape[axis_at]) // (drawn.shape[axis_at] // parts)).reshape((-1,) + (1,) * (drawn.ndim - 1 - axis_at))

    first = jax.random.permutation(rng, parts)[block_of(target)]
    far = (block_of(target) + parts // 2) % parts
    return jnp.where((block_of(source) == first) | (block_of(source) == far), factor * drawn, drawn)


def block_levels(stream_key, shape, shards, smallest, largest):
    factor_of, own = 1.0, jax.random.fold_in(stream_key, 6)
    for axis_at, shards_of in shards:
        draws = jnp.exp(jax.random.uniform(jax.random.fold_in(own, axis_at), (shards_of,), jnp.float32, smallest / len(shards), largest / len(shards)))
        factor_of = factor_of * jnp.repeat(draws, shape[axis_at] // shards_of).reshape([-1 if axis == axis_at else 1 for axis in range(len(shape))])
    return factor_of


def normal_values(own_key, shape, spread, bound, shards=(), dtype=jnp.bfloat16):
    values = spread * jax.random.normal(own_key, shape, jnp.float32)
    if shards:
        values = values * block_levels(own_key, shape, shards, -0.22, 0.18)
    return jnp.clip(values, -bound, bound).astype(dtype)


def bell_draw_with(key, extent, scale, limit, split, heavy, held_as=jnp.bfloat16):
    values = scale * jax.random.normal(key, extent, jnp.float32)
    if split:
        values = values * block_levels(key, extent, split, -0.22, 0.18)
    return jnp.clip(with_spikes(values, jax.random.fold_in(key, 3), *heavy), -limit, limit).astype(held_as)


def setup_inputs(seed: int = 0) -> dict:
    keys = jax.random.split(jax.random.key(seed), 10)
    return {
        "hidden": normal_values(keys[0], (LENGTH, D), 1.0, 6.0, ((0, 16), (1, 16))),
        "norm_gain": jnp.clip(1.0 + 0.15 * jax.random.normal(keys[1], (D,), jnp.float32), 0.25, 1.75),
        "value_weight": normal_values(keys[2], (D, D), D ** -0.5, 0.09375, ((1, 16),)),
        "gate_weight": normal_values(keys[3], (D, D), D ** -0.5, 0.09375, ((1, 16),)),
        "value_taps": normal_values(keys[4], (3, D), 0.6, 3.0, ((1, 16),), jnp.float32),
        "gate_taps": normal_values(keys[5], (3, D), 0.6, 3.0, ((1, 16),), jnp.float32),
        "rates": draw_rates(jax.random.fold_in(keys[9], 71), 0),
        "residues": normal_values(keys[7], (MODES, D), MODES ** -0.5, 1.5, ((1, 16),), jnp.float32),
        "out_weight": bell_draw_with(keys[8], (D, D), D ** -0.5, 0.125, ((0, 16),), (0, 1, 16, 2.0)),
    }


eps = 1e-05

def normalize(whole, gain):
    values = whole.astype(jnp.float32)
    scale = lax.rsqrt(lax.optimization_barrier(jnp.mean(values * values, axis=1, keepdims=True)) + eps)
    return (values * scale * gain.astype(jnp.float32)[None, :]).astype(jnp.bfloat16)

def short_filter(signal, taps):
    padded = jnp.pad(signal.astype(jnp.float32), ((1, 1), (0, 0)))
    return taps[0][None, :] * padded[:-2] + taps[1][None, :] * padded[1:-1] + taps[2][None, :] * padded[2:]

def long_conv(signal, rates, residues):
    length = signal.shape[0]
    width = math.gcd(signal.shape[1], 128)
    count = signal.shape[1] // width
    strength = residues * jnp.sqrt(rates)
    lags = jnp.arange(2 * length)
    distance = jnp.minimum(lags, 2 * length - lags).astype(jnp.float32)
    keep = (lags != length).astype(jnp.float32)
    pieces = signal.reshape(length, count, width).transpose(1, 0, 2)
    rate_parts = rates.reshape(rates.shape[0], count, width).transpose(1, 0, 2)
    strength_parts = strength.reshape(rates.shape[0], count, width).transpose(1, 0, 2)

    def one_block(packed):
        piece, rate_part, strength_part = packed
        kernel = lax.optimization_barrier(jnp.sum(strength_part[None] * jnp.exp(-rate_part[None] * distance[:, None, None]), axis=1))
        kernel = kernel * keep[:, None]
        padded = jnp.pad(piece, ((0, length), (0, 0)))
        product = jnp.fft.rfft(padded, axis=0) * jnp.fft.rfft(kernel, axis=0)
        return jnp.fft.irfft(product, n=2 * length, axis=0)[:length]
    result = lax.map(one_block, (pieces, rate_parts, strength_parts))
    return result.transpose(1, 0, 2).reshape(length, signal.shape[1])

def reference(hidden, norm_gain, value_weight, gate_weight, value_taps, gate_taps, rates, residues, out_weight):

    def branch(source):
        normed = normalize(source, norm_gain)
        values = jnp.dot(normed, value_weight, preferred_element_type=jnp.float32).astype(jnp.bfloat16)
        gates = jnp.dot(normed, gate_weight, preferred_element_type=jnp.float32).astype(jnp.bfloat16)
        smooth_values = short_filter(values, value_taps)
        smooth_gates = short_filter(gates, gate_taps)
        conv = long_conv(smooth_values, rates, residues)
        return (smooth_gates * conv).astype(jnp.bfloat16)
    forward = branch(hidden)
    backward = branch(hidden[::-1, ::-1])
    total = jnp.dot(forward, out_weight, preferred_element_type=jnp.float32)
    total = total + jnp.dot(backward, out_weight, preferred_element_type=jnp.float32)[::-1, ::-1]
    return total.astype(jnp.bfloat16)
```

```python
import functools
import jax
import jax.numpy as jnp
from jax import lax
from jax.experimental import pallas as pl
from jax.experimental.pallas import tpu as pltpu
from jax.sharding import PartitionSpec as P

eps = 1e-05
f32 = jnp.float32
bf16 = jnp.bfloat16
T = 16


def tables_kernel(rates_ref, residues_ref, pow_ref, near_ref, fore_ref, back_ref):
    rates = rates_ref[...]
    modes, chans = rates.shape
    strength = residues_ref[...] * jnp.sqrt(rates)
    for k in range(T):
        pow_ref[k] = jnp.exp(-rates * float(k))
    pow_ref[T] = jnp.exp(-rates * float(T))
    pow_ref[T + 1] = jnp.exp(rates)
    steps = lax.broadcasted_iota(jnp.int32, (T, chans), 0).astype(f32)
    total = jnp.zeros((T, chans), f32)
    for m in range(modes):
        rate = rates[m : m + 1, :]
        weight = strength[m : m + 1, :]
        fore = weight * jnp.exp(-rate * (steps + 1.0))
        fore_ref[m] = fore
        back_ref[m] = weight * jnp.exp(-rate * (float(T) - steps))
        total = total + fore
    near_ref[pl.ds(T + 1, T), :] = total
    near_ref[pl.ds(T, 1), :] = jnp.sum(strength, axis=0, keepdims=True)
    for k in range(1, T + 1):
        near_ref[pl.ds(T - k, 1), :] = total[k - 1 : k, :]


def project_kernel(
    x_ref, gain_ref, wv_ref, wg_ref, vt_ref, gt_ref, pow_ref, near_ref,
    send_ref, fore_ref, back_ref, local_ref, gates_ref,
    acc_ref, scale_ref, pad_ref, sv_ref,
):
    k = pl.program_id(0)
    blocks, rows, chans = x_ref.shape
    place = lax.axis_index("seq")
    places = lax.axis_size("seq")

    @pl.when(k == 0)
    def _():
        total = jnp.zeros((rows, chans), f32)
        for b in range(blocks):
            part = x_ref[b].astype(f32)
            total = total + part * part
        mean = jnp.sum(total, axis=1, keepdims=True) * (1.0 / (blocks * chans))
        scale_ref[...] = jnp.broadcast_to(lax.rsqrt(mean + eps), scale_ref.shape)
        acc_ref[...] = jnp.zeros_like(acc_ref)

    scale = scale_ref[:, 0:1]
    gain = gain_ref[0]
    i0 = lax.broadcasted_iota(jnp.int32, (chans, chans), 0)
    i1 = lax.broadcasted_iota(jnp.int32, (chans, chans), 1)
    flip = (i0 + i1 == chans - 1).astype(f32).astype(bf16)
    own = (x_ref[k].astype(f32) * scale * gain).astype(bf16)
    far = jnp.dot(x_ref[blocks - 1 - k], flip, preferred_element_type=f32)
    far = (far * scale * gain).astype(bf16)
    both = jnp.concatenate([own, far], axis=0)
    weight = jnp.concatenate([wv_ref[...], wg_ref[...]], axis=1)
    acc_ref[...] += jnp.dot(both, weight, preferred_element_type=f32)

    @pl.when(k == blocks - 1)
    def _():
        low_ok = (place > 0).astype(f32)
        high_ok = (place < places - 1).astype(f32)
        zeros8 = jnp.zeros((8, chans), f32)
        edges = []
        for s in range(2):
            v = acc_ref[s * rows : (s + 1) * rows, :chans].astype(bf16).astype(f32)
            pad_ref[0:8, :] = zeros8
            pad_ref[8 : 8 + rows, :] = v
            pad_ref[8 + rows : 16 + rows, :] = zeros8
            a, c = (0, 2) if s == 0 else (2, 0)
            ta, tb, tc = vt_ref[a : a + 1, :], vt_ref[1:2, :], vt_ref[c : c + 1, :]
            sv = ta * pad_ref[7 : 7 + rows, :] + tb * v + tc * pad_ref[9 : 9 + rows, :]
            sv_ref[s] = sv.reshape(rows // T, T, chans)
            low = tc * v[0:1, :] * low_ok
            high = ta * v[rows - 1 : rows, :] * high_ok
            edges.append((low, high))
            gates_ref[s] = acc_ref[s * rows : (s + 1) * rows, chans:].astype(bf16)
        tiles = rows // T
        for s in range(2):
            for g in range(chans // 128):
                lanes = slice(g * 128, (g + 1) * 128)
                low, high = edges[s][0][:, lanes], edges[s][1][:, lanes]
                inner = jnp.zeros((tiles, T, 128), f32)
                for j in range(T):
                    inner = inner + near_ref[T - j : 2 * T - j, lanes][None] * sv_ref[s, :, j : j + 1, lanes]
                local_ref[s, :, :, lanes] = inner
                fold = jnp.zeros((tiles, 16, 128), f32)
                for j in range(T):
                    fold = fold + pow_ref[T - 1 - j, :, lanes][None] * sv_ref[s, :, j : j + 1, lanes]
                jump = pow_ref[T, :, lanes]
                inverse = pow_ref[T + 1, :, lanes]
                state = jnp.broadcast_to(low, (16, 128))
                for n in range(tiles):
                    fore_ref[s, n, :, lanes] = state
                    state = jump * state + fold[n]
                ahead = state + inverse * high
                fold = jnp.zeros((tiles, 16, 128), f32)
                for j in range(T):
                    fold = fold + pow_ref[j, :, lanes][None] * sv_ref[s, :, j : j + 1, lanes]
                state = jnp.broadcast_to(high, (16, 128))
                for n in reversed(range(tiles)):
                    back_ref[s, n, :, lanes] = state
                    state = jump * state + fold[n]
                behind = state + inverse * low
                wide = slice(s * chans + g * 128, s * chans + (g + 1) * 128)
                first = jnp.broadcast_to(gates_ref[s, 0:1, lanes].astype(f32), (8, 128))
                last = jnp.broadcast_to(gates_ref[s, rows - 1 : rows, lanes].astype(f32), (8, 128))

                for i in range(places):
                    later = i > place
                    send_ref[i, 0:16, wide] = jnp.where(later, ahead, behind)
                    send_ref[i, 16:24, wide] = jnp.where(later, last, first)


def output_kernel(
    recv_ref, fore_ref, back_ref, local_ref, gates_ref, gt_ref, rates_ref, spread_f_ref, spread_b_ref,
    near_w_ref, far_w_ref, out_ref, z_ref, pad_ref, st_ref,
):
    k = pl.program_id(0)
    rows = gates_ref.shape[1]
    chans = gates_ref.shape[2]
    tiles = rows // T
    place = lax.axis_index("seq")
    places = lax.axis_size("seq")

    @pl.when(k == 0)
    def _():
        low_ok = (place > 0).astype(f32)
        high_ok = (place < places - 1).astype(f32)
        below = jnp.maximum(place - 1, 0)
        above = jnp.minimum(place + 1, places - 1)
        for s in range(2):
            wide = slice(s * chans, (s + 1) * chans)
            g = gates_ref[s].astype(f32)
            pad_ref[0:8, :] = recv_ref[below, 16:24, wide] * low_ok
            pad_ref[8 : 8 + rows, :] = g
            pad_ref[8 + rows : 16 + rows, :] = recv_ref[above, 16:24, wide] * high_ok
            a, c = (0, 2) if s == 0 else (2, 0)
            ta, tb, tc = gt_ref[a : a + 1, :], gt_ref[1:2, :], gt_ref[c : c + 1, :]
            sg = ta * pad_ref[7 : 7 + rows, :] + tb * g + tc * pad_ref[9 : 9 + rows, :]
            for g2 in range(chans // 128):
                lanes = slice(g2 * 128, (g2 + 1) * 128)
                wide = slice(s * chans + g2 * 128, s * chans + (g2 + 1) * 128)
                rates = rates_ref[:, lanes]
                hop = jnp.exp(-rates * float(rows))
                jump = jnp.exp(-rates * float(T))
                carry_f = jnp.zeros((16, 128), f32)
                carry_b = jnp.zeros((16, 128), f32)
                for j in range(places):
                    r = places - 1 - j
                    carry_f = jnp.where(j < place, carry_f * hop + recv_ref[j, 0:16, wide], carry_f)
                    carry_b = jnp.where(r > place, carry_b * hop + recv_ref[r, 0:16, wide], carry_b)
                for n in range(tiles):
                    m = tiles - 1 - n
                    st_ref[0, n] = fore_ref[s, n, :, lanes] + carry_f
                    st_ref[1, m] = back_ref[s, m, :, lanes] + carry_b
                    carry_f = carry_f * jump
                    carry_b = carry_b * jump
                conv = local_ref[s, :, :, lanes]
                for m in range(16):
                    conv = conv + spread_f_ref[m, :, lanes][None] * st_ref[0, :, m : m + 1, :]
                for m in range(16):
                    conv = conv + spread_b_ref[m, :, lanes][None] * st_ref[1, :, m : m + 1, :]
                z_ref[:, wide] = (sg[:, lanes] * conv.reshape(rows, 128)).astype(bf16)

    i0 = lax.broadcasted_iota(jnp.int32, (chans, chans), 0)
    i1 = lax.broadcasted_iota(jnp.int32, (chans, chans), 1)
    flip = (i0 + i1 == chans - 1).astype(f32).astype(bf16)
    far = jnp.dot(far_w_ref[...], flip, preferred_element_type=f32).astype(bf16)
    weight = jnp.concatenate([near_w_ref[...], far], axis=0)
    out_ref[0] = jnp.dot(z_ref[...], weight, preferred_element_type=f32).astype(bf16)


def whole(shape):
    return pl.BlockSpec(shape, lambda *_: (0,) * len(shape))


def body(
    hidden, norm_gain, value_weight, gate_weight, value_taps, gate_taps, rates, residues, out_weight
):
    rows, chans = hidden.shape
    tp = lax.axis_size("tp")
    places = lax.axis_size("seq")
    modes = rates.shape[0]
    tiles = rows // T
    shape = jax.ShapeDtypeStruct
    params = pltpu.CompilerParams(vmem_limit_bytes=48 << 20)

    powers, near, spread_f, spread_b = pl.pallas_call(
        tables_kernel,
        out_shape=(
            shape((T + 2, modes, chans), f32),
            shape((2 * T + 8, chans), f32),
            shape((modes, T, chans), f32),
            shape((modes, T, chans), f32),
        ),
        compiler_params=params,
        name="tables",
    )(rates, residues)

    blocks = lax.all_to_all(
        jnp.broadcast_to(hidden[None], (tp, rows, chans)), "tp", split_axis=0, concat_axis=0
    )
    gain = norm_gain.reshape(tp, 1, chans)
    send, fore, back, local, gates = pl.pallas_call(
        project_kernel,
        grid=(tp,),
        in_specs=[
            whole((tp, rows, chans)),
            pl.BlockSpec((1, 1, chans), lambda k: (k, 0, 0)),
            pl.BlockSpec((chans, chans), lambda k: (k, 0)),
            pl.BlockSpec((chans, chans), lambda k: (k, 0)),
            whole(value_taps.shape),
            whole(gate_taps.shape),
            whole(powers.shape),
            whole(near.shape),
        ],
        out_specs=[
            whole((places, 24, 2 * chans)),
            whole((2, tiles, modes, chans)),
            whole((2, tiles, modes, chans)),
            whole((2, tiles, T, chans)),
            whole((2, rows, chans)),
        ],
        out_shape=(
            shape((places, 24, 2 * chans), f32),
            shape((2, tiles, modes, chans), f32),
            shape((2, tiles, modes, chans), f32),
            shape((2, tiles, T, chans), f32),
            shape((2, rows, chans), bf16),
        ),
        scratch_shapes=[
            pltpu.VMEM((2 * rows, 2 * chans), f32),
            pltpu.VMEM((rows, 128), f32),
            pltpu.VMEM((rows + 16, chans), f32),
            pltpu.VMEM((2, tiles, T, chans), f32),
        ],
        compiler_params=params,
        name="project",
    )(blocks, gain, value_weight, gate_weight, value_taps, gate_taps, powers, near)

    recv = lax.all_to_all(send, "seq", split_axis=0, concat_axis=0)

    partial = pl.pallas_call(
        output_kernel,
        grid=(tp,),
        in_specs=[
            whole(recv.shape),
            whole(fore.shape),
            whole(back.shape),
            whole(local.shape),
            whole(gates.shape),
            whole(gate_taps.shape),
            whole(rates.shape),
            whole(spread_f.shape),
            whole(spread_b.shape),
            pl.BlockSpec((chans, chans), lambda k: (0, k)),
            pl.BlockSpec((chans, chans), lambda k: (0, tp - 1 - k)),
        ],
        out_specs=pl.BlockSpec((1, rows, chans), lambda k: (k, 0, 0)),
        out_shape=shape((tp, rows, chans), bf16),
        scratch_shapes=[
            pltpu.VMEM((rows, 2 * chans), bf16),
            pltpu.VMEM((rows + 16, chans), f32),
            pltpu.VMEM((2, tiles, modes, 128), f32),
        ],
        compiler_params=params,
        name="output",
    )(recv, fore, back, local, gates, gate_taps, rates, spread_f, spread_b, out_weight, out_weight)

    parts = lax.all_to_all(partial, "tp", split_axis=0, concat_axis=0)
    return jnp.sum(parts.astype(f32), axis=0).astype(bf16)


def solution(mesh):
    in_specs = (
        P("seq", "tp"),
        P(),
        P(None, "tp"),
        P(None, "tp"),
        P(None, "tp"),
        P(None, "tp"),
        P(None, "tp"),
        P(None, "tp"),
        P("tp", None),
    )
    out_specs = P("seq", "tp")
    return jax.shard_map(body, mesh=mesh, in_specs=in_specs, out_specs=out_specs, check_vma=False)
```

```python
import functools
import jax
import jax.numpy as jnp
from jax import lax
from jax.experimental import pallas as pl
from jax.experimental.pallas import tpu as pltpu
from jax.sharding import PartitionSpec as P

eps = 1e-05
f32 = jnp.float32
bf16 = jnp.bfloat16
T = 16


def tables_kernel(rates_ref, residues_ref, pow_ref, near_ref, fore_ref, back_ref):
    rates = rates_ref[...]
    modes, chans = rates.shape
    strength = residues_ref[...] * jnp.sqrt(rates)
    for k in range(T):
        pow_ref[k] = jnp.exp(-rates * float(k))
    pow_ref[T] = jnp.exp(-rates * float(T))
    pow_ref[T + 1] = jnp.exp(rates)
    steps = lax.broadcasted_iota(jnp.int32, (T, chans), 0).astype(f32)
    total = jnp.zeros((T, chans), f32)
    for m in range(modes):
        rate = rates[m : m + 1, :]
        weight = strength[m : m + 1, :]
        fore = weight * jnp.exp(-rate * (steps + 1.0))
        fore_ref[m] = fore
        back_ref[m] = weight * jnp.exp(-rate * (float(T) - steps))
        total = total + fore
    near_ref[pl.ds(T + 1, T), :] = total
    near_ref[pl.ds(T, 1), :] = jnp.sum(strength, axis=0, keepdims=True)
    for k in range(1, T + 1):
        near_ref[pl.ds(T - k, 1), :] = total[k - 1 : k, :]


def prepare_kernel(wv_ref, wg_ref, gain_ref, wo_ref, own_ref, far_ref, back_ref):
    chans = wo_ref.shape[0]
    i0 = lax.broadcasted_iota(jnp.int32, (chans, chans), 0)
    i1 = lax.broadcasted_iota(jnp.int32, (chans, chans), 1)
    flip = (i0 + i1 == chans - 1).astype(f32).astype(bf16)
    rows = jnp.broadcast_to(gain_ref[0], (chans, chans))
    gain = jnp.sum(jnp.where(i0 == i1, rows, 0.0), axis=1, keepdims=True)
    for n, ref in enumerate((wv_ref, wg_ref)):
        scaled = (ref[...].astype(f32) * gain).astype(bf16)
        own_ref[n] = scaled
        far_ref[n] = jnp.dot(flip, scaled, preferred_element_type=f32).astype(bf16)
    back_ref[...] = jnp.dot(wo_ref[...], flip, preferred_element_type=f32).astype(bf16)


def matmul_step(x_ref, own_ref, far_ref, acc_ref):
    blocks, rows, chans = x_ref.shape
    x = jnp.concatenate([x_ref[b] for b in range(blocks)], axis=1)
    first = jnp.dot(x, own_ref[0], preferred_element_type=f32)
    second = jnp.dot(x, far_ref[0], preferred_element_type=f32)
    k = pl.program_id(0)

    @pl.when(k == 0)
    def _():
        acc_ref[:, :chans] = first
        acc_ref[:, chans:] = second

    @pl.when(k > 0)
    def _():
        acc_ref[:, :chans] += first
        acc_ref[:, chans:] += second


def values_kernel(
    x_ref, own_ref, far_ref, vt_ref, pow_ref,
    send_ref, fore_ref, back_ref, sv_ref, scale_ref,
    acc_ref, sq_ref, pad_ref,
):
    k = pl.program_id(0)
    steps = pl.num_programs(0)
    blocks, rows, chans = x_ref.shape
    place = lax.axis_index("seq")
    places = lax.axis_size("seq")
    matmul_step(x_ref, own_ref, far_ref, acc_ref)
    total = jnp.zeros((rows, chans), f32)
    for b in range(blocks):
        part = x_ref[b].astype(f32)
        total = total + part * part

    @pl.when(k == 0)
    def _():
        sq_ref[...] = total

    @pl.when(k > 0)
    def _():
        sq_ref[...] += total

    @pl.when(k == steps - 1)
    def _():
        mean = jnp.sum(sq_ref[...], axis=1, keepdims=True) * (1.0 / (steps * blocks * chans))
        scale = lax.rsqrt(mean + eps)
        scale_ref[...] = jnp.broadcast_to(scale, scale_ref.shape)
        low_ok = (place > 0).astype(f32)
        high_ok = (place < places - 1).astype(f32)
        zeros8 = jnp.zeros((8, chans), f32)
        tiles = rows // T
        for s in range(2):
            v = acc_ref[:, s * chans : (s + 1) * chans] * scale
            pad_ref[0:8, :] = zeros8
            pad_ref[8 : 8 + rows, :] = v
            pad_ref[8 + rows : 16 + rows, :] = zeros8
            a, c = (0, 2) if s == 0 else (2, 0)
            ta, tb, tc = vt_ref[a : a + 1, :], vt_ref[1:2, :], vt_ref[c : c + 1, :]
            sv = ta * pad_ref[7 : 7 + rows, :] + tb * v + tc * pad_ref[9 : 9 + rows, :]
            sv_ref[s] = sv.reshape(tiles, T, chans)
            all_low = tc * v[0:1, :] * low_ok
            all_high = ta * v[rows - 1 : rows, :] * high_ok
            for g in range(chans // 128):
                lanes = slice(g * 128, (g + 1) * 128)
                low, high = all_low[:, lanes], all_high[:, lanes]
                jump = pow_ref[T, :, lanes]
                inverse = pow_ref[T + 1, :, lanes]
                fold = jnp.zeros((tiles, 16, 128), f32)
                for j in range(T):
                    fold = fold + pow_ref[T - 1 - j, :, lanes][None] * sv_ref[s, :, j : j + 1, lanes]
                state = jnp.broadcast_to(low, (16, 128))
                for n in range(tiles):
                    fore_ref[s, n, :, lanes] = state
                    state = jump * state + fold[n]
                ahead = state + inverse * high
                fold = jnp.zeros((tiles, 16, 128), f32)
                for j in range(T):
                    fold = fold + pow_ref[j, :, lanes][None] * sv_ref[s, :, j : j + 1, lanes]
                state = jnp.broadcast_to(high, (16, 128))
                for n in reversed(range(tiles)):
                    back_ref[s, n, :, lanes] = state
                    state = jump * state + fold[n]
                behind = state + inverse * low
                wide = slice(s * chans + g * 128, s * chans + (g + 1) * 128)
                for i in range(places):
                    send_ref[i, :, wide] = jnp.where(i > place, ahead, behind)


def gates_kernel(x_ref, own_ref, far_ref, scale_ref, gates_ref, first_ref, last_ref, acc_ref):
    k = pl.program_id(0)
    steps = pl.num_programs(0)
    rows = x_ref.shape[1]
    matmul_step(x_ref, own_ref, far_ref, acc_ref)

    @pl.when(k == steps - 1)
    def _():
        gates = acc_ref[...] * scale_ref[:, 0:1]
        gates_ref[...] = gates
        first_ref[...] = gates[0:8, :]
        last_ref[...] = gates[rows - 8 : rows, :]


def near_kernel(sv_ref, near_ref, local_ref):
    tiles = sv_ref.shape[1]
    chans = sv_ref.shape[3]
    for s in range(2):
        for g in range(chans // 128):
            lanes = slice(g * 128, (g + 1) * 128)
            inner = jnp.zeros((tiles, T, 128), f32)
            for j in range(T):
                inner = inner + near_ref[T - j : 2 * T - j, lanes][None] * sv_ref[s, :, j : j + 1, lanes]
            local_ref[s, :, :, lanes] = inner


def output_kernel(
    recv_ref, fore_ref, back_ref, local_ref, gates_ref, above_ref, below_ref, gt_ref, rates_ref,
    spread_f_ref, spread_b_ref, near_w_ref, far_w_ref, out_ref, z_ref, pad_ref, st_ref,
):
    k = pl.program_id(0)
    rows = gates_ref.shape[0]
    chans = gates_ref.shape[1] // 2
    tiles = rows // T
    place = lax.axis_index("seq")
    places = lax.axis_size("seq")

    @pl.when(k == 0)
    def _():
        for s in range(2):
            wide = slice(s * chans, (s + 1) * chans)
            g = gates_ref[:, wide]
            pad_ref[0:8, :] = below_ref[:, wide]
            pad_ref[8 : 8 + rows, :] = g
            pad_ref[8 + rows : 16 + rows, :] = above_ref[:, wide]
            a, c = (0, 2) if s == 0 else (2, 0)
            ta, tb, tc = gt_ref[a : a + 1, :], gt_ref[1:2, :], gt_ref[c : c + 1, :]
            sg = ta * pad_ref[7 : 7 + rows, :] + tb * g + tc * pad_ref[9 : 9 + rows, :]
            for g2 in range(chans // 128):
                lanes = slice(g2 * 128, (g2 + 1) * 128)
                wide = slice(s * chans + g2 * 128, s * chans + (g2 + 1) * 128)
                rates = rates_ref[:, lanes]
                hop = jnp.exp(-rates * float(rows))
                jump = jnp.exp(-rates * float(T))
                carry_f = jnp.zeros((16, 128), f32)
                carry_b = jnp.zeros((16, 128), f32)
                for j in range(places):
                    r = places - 1 - j
                    carry_f = jnp.where(j < place, carry_f * hop + recv_ref[j, :, wide], carry_f)
                    carry_b = jnp.where(r > place, carry_b * hop + recv_ref[r, :, wide], carry_b)
                for n in range(tiles):
                    m = tiles - 1 - n
                    st_ref[0, n] = fore_ref[s, n, :, lanes] + carry_f
                    st_ref[1, m] = back_ref[s, m, :, lanes] + carry_b
                    carry_f = carry_f * jump
                    carry_b = carry_b * jump
                conv = local_ref[s, :, :, lanes]
                for m in range(16):
                    conv = conv + spread_f_ref[m, :, lanes][None] * st_ref[0, :, m : m + 1, :]
                for m in range(16):
                    conv = conv + spread_b_ref[m, :, lanes][None] * st_ref[1, :, m : m + 1, :]
                z_ref[:, wide] = (sg[:, lanes] * conv.reshape(rows, 128)).astype(bf16)

    out = jnp.dot(z_ref[:, :chans], near_w_ref[...], preferred_element_type=f32)
    out = out + jnp.dot(z_ref[:, chans:], far_w_ref[...], preferred_element_type=f32)
    for b in range(out_ref.shape[0]):
        out_ref[b] = out[:, b * chans : (b + 1) * chans].astype(bf16)


def far_memory(*arrays):
    return [pltpu.with_memory_space_constraint(a, pltpu.HBM) for a in arrays]


def whole(shape):
    return pl.BlockSpec(shape, lambda *_: (0,) * len(shape))


def body(
    hidden, norm_gain, value_weight, gate_weight, value_taps, gate_taps, rates, residues, out_weight
):
    rows, chans = hidden.shape
    tp = lax.axis_size("tp")
    places = lax.axis_size("seq")
    modes = rates.shape[0]
    tiles = rows // T
    width = value_weight.shape[0]
    shape = pltpu.HBM
    params = pltpu.CompilerParams(vmem_limit_bytes=14 << 20)
    square = pl.BlockSpec((chans, chans), lambda k: (k, 0))

    blocks = lax.all_to_all(
        jnp.broadcast_to(hidden[None], (tp, rows, chans)), "tp", split_axis=0, concat_axis=0
    )

    powers, near, spread_f, spread_b = pl.pallas_call(
        tables_kernel,
        out_shape=(
            shape((T + 2, modes, chans), f32),
            shape((2 * T + 8, chans), f32),
            shape((modes, T, chans), f32),
            shape((modes, T, chans), f32),
        ),
        compiler_params=params,
        name="tables",
    )(rates, residues)
    own_w, far_w, back_w = pl.pallas_call(
        prepare_kernel,
        grid=(tp,),
        in_specs=[
            square,
            square,
            pl.BlockSpec((1, 1, chans), lambda k: (k, 0, 0)),
            pl.BlockSpec((chans, chans), lambda k: (0, k)),
        ],
        out_specs=[
            pl.BlockSpec((2, chans, chans), lambda k: (0, k, 0)),
            pl.BlockSpec((2, chans, chans), lambda k: (0, tp - 1 - k, 0)),
            pl.BlockSpec((chans, chans), lambda k: (0, tp - 1 - k)),
        ],
        out_shape=(
            shape((2, width, chans), bf16),
            shape((2, width, chans), bf16),
            shape((chans, width), bf16),
        ),
        compiler_params=params,
        name="prepare",
    )(*far_memory(value_weight, gate_weight), norm_gain.reshape(tp, 1, chans), *far_memory(out_weight))

    group = 4
    steps = tp // group
    x_spec = pl.BlockSpec((group, rows, chans), lambda k: (k, 0, 0))

    def w_spec(n):
        return pl.BlockSpec((1, group * chans, chans), lambda k: (n, k, 0))

    send, fore, back, sv, scale = pl.pallas_call(
        values_kernel,
        grid=(steps,),
        in_specs=[x_spec, w_spec(0), w_spec(0), whole(value_taps.shape), whole(powers.shape)],
        out_specs=[
            whole((places, modes, 2 * chans)),
            whole((2, tiles, modes, chans)),
            whole((2, tiles, modes, chans)),
            whole((2, tiles, T, chans)),
            whole((rows, 128)),
        ],
        out_shape=(
            shape((places, modes, 2 * chans), f32),
            shape((2, tiles, modes, chans), f32),
            shape((2, tiles, modes, chans), f32),
            shape((2, tiles, T, chans), f32),
            shape((rows, 128), f32),
        ),
        scratch_shapes=[
            pltpu.VMEM((rows, 2 * chans), f32),
            pltpu.VMEM((rows, chans), f32),
            pltpu.VMEM((rows + 16, chans), f32),
        ],
        compiler_params=params,
        name="values",
    )(blocks, *far_memory(own_w, far_w), value_taps, *far_memory(powers))

    recv = lax.all_to_all(send, "seq", split_axis=0, concat_axis=0)

    gates, first, last = pl.pallas_call(
        gates_kernel,
        grid=(steps,),
        in_specs=[x_spec, w_spec(1), w_spec(1), whole((rows, 128))],
        out_specs=[whole((rows, 2 * chans)), whole((8, 2 * chans)), whole((8, 2 * chans))],
        out_shape=(
            shape((rows, 2 * chans), f32),
            shape((8, 2 * chans), f32),
            shape((8, 2 * chans), f32),
        ),
        scratch_shapes=[pltpu.VMEM((rows, 2 * chans), f32)],
        compiler_params=params,
        name="gates",
    )(blocks, *far_memory(own_w, far_w, scale))
    up = [(i, i + 1) for i in range(places - 1)]
    below = lax.ppermute(last, "seq", up)
    above = lax.ppermute(first, "seq", [(b, a) for a, b in up])

    local = pl.pallas_call(
        near_kernel,
        out_shape=shape((2, tiles, T, chans), f32),
        compiler_params=params,
        name="near",
    )(*far_memory(sv, near))

    partial = pl.pallas_call(
        output_kernel,
        grid=(steps,),
        in_specs=[
            whole(recv.shape),
            whole(fore.shape),
            whole(back.shape),
            whole(local.shape),
            whole(gates.shape),
            whole(above.shape),
            whole(below.shape),
            whole(gate_taps.shape),
            whole(rates.shape),
            whole(spread_f.shape),
            whole(spread_b.shape),
            pl.BlockSpec((chans, group * chans), lambda k: (0, k)),
            pl.BlockSpec((chans, group * chans), lambda k: (0, k)),
        ],
        out_specs=pl.BlockSpec((group, rows, chans), lambda k: (k, 0, 0)),
        out_shape=jax.ShapeDtypeStruct((tp, rows, chans), bf16),
        scratch_shapes=[
            pltpu.VMEM((rows, 2 * chans), bf16),
            pltpu.VMEM((rows + 16, chans), f32),
            pltpu.VMEM((2, tiles, modes, 128), f32),
        ],
        compiler_params=params,
        name="output",
    )(
        recv, *far_memory(fore, back, local, gates), above, below, gate_taps, rates,
        *far_memory(spread_f, spread_b, out_weight, back_w),
    )

    parts = lax.all_to_all(partial, "tp", split_axis=0, concat_axis=0)
    return jnp.sum(parts.astype(f32), axis=0).astype(bf16)


def solution(mesh):
    in_specs = (
        P("seq", "tp"),
        P(),
        P(None, "tp"),
        P(None, "tp"),
        P(None, "tp"),
        P(None, "tp"),
        P(None, "tp"),
        P(None, "tp"),
        P("tp", None),
    )
    out_specs = P("seq", "tp")
    return jax.shard_map(body, mesh=mesh, in_specs=in_specs, out_specs=out_specs, check_vma=False)
```

```python
import functools
import jax
import jax.numpy as jnp
from jax import lax
from jax.experimental import pallas as pl
from jax.experimental.pallas import tpu as pltpu
from jax.sharding import PartitionSpec as P

eps = 1e-05
f32 = jnp.float32
bf16 = jnp.bfloat16
T = 16


def tables_kernel(rates_ref, residues_ref, pow_ref, near_ref, fore_ref, back_ref):
    rates = rates_ref[...]
    modes, chans = rates.shape
    strength = residues_ref[...] * jnp.sqrt(rates)
    for k in range(T):
        pow_ref[k] = jnp.exp(-rates * float(k))
    pow_ref[T] = jnp.exp(-rates * float(T))
    pow_ref[T + 1] = jnp.exp(rates)
    steps = lax.broadcasted_iota(jnp.int32, (T, chans), 0).astype(f32)
    total = jnp.zeros((T, chans), f32)
    for m in range(modes):
        rate = rates[m : m + 1, :]
        weight = strength[m : m + 1, :]
        fore = weight * jnp.exp(-rate * (steps + 1.0))
        fore_ref[m] = fore
        back_ref[m] = weight * jnp.exp(-rate * (float(T) - steps))
        total = total + fore
    near_ref[pl.ds(T + 1, T), :] = total
    near_ref[pl.ds(T, 1), :] = jnp.sum(strength, axis=0, keepdims=True)
    for k in range(1, T + 1):
        near_ref[pl.ds(T - k, 1), :] = total[k - 1 : k, :]


def reversal(n):
    i0 = lax.broadcasted_iota(jnp.int32, (n, n), 0)
    i1 = lax.broadcasted_iota(jnp.int32, (n, n), 1)
    return (i0 + i1 == n - 1).astype(f32).astype(bf16)


def shard_at(place, column, hop, tp):
    ring = tp // 2
    return ((place // ring + column) % 2) * ring + (place % ring + hop + ring) % ring


def rows_of(block, size):
    return pl.ds(pl.multiple_of(block * size, size), size)


def accumulate(slots, x_refs, gain_ref, weights, x_buf, w_buf, sems, acc_ref, sq_ref, fresh):
    tp = lax.axis_size("tp")
    place = lax.axis_index("tp")
    rows, chans = x_buf.shape[1:]
    copies = []
    for n, (array, entry, column, hop) in enumerate(slots):
        block = shard_at(place, column, hop, tp)
        source = x_refs[array] if entry is None else x_refs[array].at[entry]
        group = [pltpu.make_async_copy(source, x_buf.at[n], sems.at[n, 0])]
        for w, ref in enumerate(weights):
            lanes = pl.ds(w * chans, chans)
            group.append(
                pltpu.make_async_copy(ref.at[rows_of(block, chans), :], w_buf.at[n, 0, :, lanes], sems.at[n, 1 + w])
            )
            group.append(
                pltpu.make_async_copy(
                    ref.at[rows_of(tp - 1 - block, chans), :], w_buf.at[n, 1, :, lanes], sems.at[n, 3 + w]
                )
            )
        for copy in group:
            copy.start()
        copies.append(group)
    flip = reversal(chans)
    wide = w_buf.shape[3]
    for n, (array, entry, column, hop) in enumerate(slots):
        block = shard_at(place, column, hop, tp)
        for copy in copies[n]:
            copy.wait()
        x = x_buf[n]
        part = x.astype(f32)
        mirrored = jnp.dot(x, flip, preferred_element_type=f32)
        own = (part * gain_ref[block]).astype(bf16)
        far = (mirrored * gain_ref[tp - 1 - block]).astype(bf16)
        first = jnp.dot(own, w_buf[n, 0], preferred_element_type=f32)
        second = jnp.dot(far, w_buf[n, 1], preferred_element_type=f32)
        if fresh and n == 0:
            sq_ref[...] = part * part
            acc_ref[0] = first
            acc_ref[1] = second
        else:
            sq_ref[...] += part * part
            acc_ref[0] += first
            acc_ref[1] += second


def early_kernel(slots, arrays, fresh, *refs):
    x_refs, refs = refs[:arrays], refs[arrays:]
    gain_ref, wv_ref, wg_ref, refs = refs[0], refs[1], refs[2], refs[3:]
    if not fresh:
        acc_in, sq_in, refs = refs[0], refs[1], refs[2:]
    acc_ref, sq_ref, x_buf, w_buf, sems = refs
    if not fresh:
        acc_ref[...] = acc_in[...]
        sq_ref[...] = sq_in[...]
    accumulate(slots, x_refs, gain_ref, (wv_ref, wg_ref), x_buf, w_buf, sems, acc_ref, sq_ref, fresh)


def states_kernel(slots, arrays, *refs):
    x_refs, refs = refs[:arrays], refs[arrays:]
    gain_ref, wv_ref, wg_ref, acc_in, sq_in, vt_ref, pow_ref, refs = *refs[:7], refs[7:]
    send_ref, fore_ref, back_ref, sv_ref, gates_ref, first_ref, last_ref, refs = *refs[:7], refs[7:]
    acc_ref, sq_ref, pad_ref, x_buf, w_buf, sems = refs
    acc_ref[...] = acc_in[...]
    sq_ref[...] = sq_in[...]
    accumulate(slots, x_refs, gain_ref, (wv_ref, wg_ref), x_buf, w_buf, sems, acc_ref, sq_ref, False)
    rows, chans = sq_ref.shape
    place = lax.axis_index("seq")
    places = lax.axis_size("seq")
    mean = jnp.sum(sq_ref[...], axis=1, keepdims=True) * (1.0 / (lax.axis_size("tp") * chans))
    scale = lax.rsqrt(mean + eps)
    low_ok = (place > 0).astype(f32)
    high_ok = (place < places - 1).astype(f32)
    zeros8 = jnp.zeros((8, chans), f32)
    tiles = rows // T
    for s in range(2):
        strand = slice(s * chans, (s + 1) * chans)
        gates = acc_ref[s, :, chans:] * scale
        gates_ref[:, strand] = gates
        first_ref[:, strand] = gates[0:8, :]
        last_ref[:, strand] = gates[rows - 8 : rows, :]
        v = acc_ref[s, :, :chans] * scale
        pad_ref[0:8, :] = zeros8
        pad_ref[8 : 8 + rows, :] = v
        pad_ref[8 + rows : 16 + rows, :] = zeros8
        a, c = (0, 2) if s == 0 else (2, 0)
        ta, tb, tc = vt_ref[a : a + 1, :], vt_ref[1:2, :], vt_ref[c : c + 1, :]
        sv = ta * pad_ref[7 : 7 + rows, :] + tb * v + tc * pad_ref[9 : 9 + rows, :]
        sv_ref[s] = sv.reshape(tiles, T, chans)
        all_low = tc * v[0:1, :] * low_ok
        all_high = ta * v[rows - 1 : rows, :] * high_ok
        for g in range(chans // 128):
            lanes = slice(g * 128, (g + 1) * 128)
            low, high = all_low[:, lanes], all_high[:, lanes]
            jump = pow_ref[T, :, lanes]
            inverse = pow_ref[T + 1, :, lanes]
            fold = jnp.zeros((tiles, 16, 128), f32)
            for j in range(T):
                fold = fold + pow_ref[T - 1 - j, :, lanes][None] * sv_ref[s, :, j : j + 1, lanes]
            state = jnp.broadcast_to(low, (16, 128))
            for n in range(tiles):
                fore_ref[s, n, :, lanes] = state
                state = jump * state + fold[n]
            ahead = state + inverse * high
            fold = jnp.zeros((tiles, 16, 128), f32)
            for j in range(T):
                fold = fold + pow_ref[j, :, lanes][None] * sv_ref[s, :, j : j + 1, lanes]
            state = jnp.broadcast_to(high, (16, 128))
            for n in reversed(range(tiles)):
                back_ref[s, n, :, lanes] = state
                state = jump * state + fold[n]
            behind = state + inverse * low
            wide = slice(s * chans + g * 128, s * chans + (g + 1) * 128)
            for i in range(places):
                send_ref[i, :, wide] = jnp.where(i > place, ahead, behind)


def near_kernel(sv_ref, near_ref, local_ref):
    tiles = sv_ref.shape[1]
    chans = sv_ref.shape[3]
    for s in range(2):
        for g in range(chans // 128):
            lanes = slice(g * 128, (g + 1) * 128)
            inner = jnp.zeros((tiles, T, 128), f32)
            for j in range(T):
                inner = inner + near_ref[T - j : 2 * T - j, lanes][None] * sv_ref[s, :, j : j + 1, lanes]
            local_ref[s, :, :, lanes] = inner


def fetch_columns(chunks, wo_ref, w_buf, sems):
    tp = lax.axis_size("tp")
    place = lax.axis_index("tp")
    chans = w_buf.shape[2]
    copies = []
    for n, (column, hop) in enumerate(chunks):
        block = shard_at(place, column, hop, tp)
        pair = (
            pltpu.make_async_copy(wo_ref.at[:, rows_of(block, chans)], w_buf.at[n, 0], sems.at[n, 0]),
            pltpu.make_async_copy(wo_ref.at[:, rows_of(tp - 1 - block, chans)], w_buf.at[n, 1], sems.at[n, 1]),
        )
        for copy in pair:
            copy.start()
        copies.append(pair)
    return copies


def partial_chunk(n, copies, z_ref, w_buf, flip):
    chans = w_buf.shape[2]
    for copy in copies[n]:
        copy.wait()
    far = jnp.dot(w_buf[n, 1], flip, preferred_element_type=f32).astype(bf16)
    out = jnp.dot(z_ref[:, :chans], w_buf[n, 0], preferred_element_type=f32)
    return out + jnp.dot(z_ref[:, chans:], far, preferred_element_type=f32)


def gated_kernel(
    chunks, recv_ref, fore_ref, back_ref, local_ref, gates_ref, above_ref, below_ref, gt_ref, rates_ref,
    spread_f_ref, spread_b_ref, wo_ref, z_ref, *refs,
):
    outs, (pad_ref, st_ref, w_buf, sems) = refs[: len(chunks)], refs[len(chunks) :]
    rows = gates_ref.shape[0]
    chans = gates_ref.shape[1] // 2
    tiles = rows // T
    place = lax.axis_index("seq")
    places = lax.axis_size("seq")
    copies = fetch_columns(chunks, wo_ref, w_buf, sems)
    for s in range(2):
        wide = slice(s * chans, (s + 1) * chans)
        g = gates_ref[:, wide]
        pad_ref[0:8, :] = below_ref[:, wide]
        pad_ref[8 : 8 + rows, :] = g
        pad_ref[8 + rows : 16 + rows, :] = above_ref[:, wide]
        a, c = (0, 2) if s == 0 else (2, 0)
        ta, tb, tc = gt_ref[a : a + 1, :], gt_ref[1:2, :], gt_ref[c : c + 1, :]
        sg = ta * pad_ref[7 : 7 + rows, :] + tb * g + tc * pad_ref[9 : 9 + rows, :]
        for g2 in range(chans // 128):
            lanes = slice(g2 * 128, (g2 + 1) * 128)
            wide = slice(s * chans + g2 * 128, s * chans + (g2 + 1) * 128)
            rates = rates_ref[:, lanes]
            hop = jnp.exp(-rates * float(rows))
            jump = jnp.exp(-rates * float(T))
            carry_f = jnp.zeros((16, 128), f32)
            carry_b = jnp.zeros((16, 128), f32)
            for j in range(places):
                r = places - 1 - j
                carry_f = jnp.where(j < place, carry_f * hop + recv_ref[j, :, wide], carry_f)
                carry_b = jnp.where(r > place, carry_b * hop + recv_ref[r, :, wide], carry_b)
            for n in range(tiles):
                m = tiles - 1 - n
                st_ref[0, n] = fore_ref[s, n, :, lanes] + carry_f
                st_ref[1, m] = back_ref[s, m, :, lanes] + carry_b
                carry_f = carry_f * jump
                carry_b = carry_b * jump
            conv = local_ref[s, :, :, lanes]
            for m in range(16):
                conv = conv + spread_f_ref[m, :, lanes][None] * st_ref[0, :, m : m + 1, :]
            for m in range(16):
                conv = conv + spread_b_ref[m, :, lanes][None] * st_ref[1, :, m : m + 1, :]
            z_ref[:, wide] = (sg[:, lanes] * conv.reshape(rows, 128)).astype(bf16)
    flip = reversal(chans)
    for n, ref in enumerate(outs):
        ref[...] = partial_chunk(n, copies, z_ref, w_buf, flip).astype(bf16)


def rest_kernel(chunks, z_ref, wo_ref, *refs):
    outs, (w_buf, sems) = refs[:-2], refs[-2:]
    copies = fetch_columns(chunks, wo_ref, w_buf, sems)
    flip = reversal(w_buf.shape[2])
    for n in range(len(chunks)):
        outs[n // 2][n % 2] = partial_chunk(n, copies, z_ref, w_buf, flip).astype(bf16)


def far_memory(*arrays):
    return [pltpu.with_memory_space_constraint(a, pltpu.HBM) for a in arrays]


def whole(shape):
    return pl.BlockSpec(shape, lambda *_: (0,) * len(shape))


remote = pl.BlockSpec(memory_space=pl.ANY)


def body(
    hidden, norm_gain, value_weight, gate_weight, value_taps, gate_taps, rates, residues, out_weight
):
    rows, chans = hidden.shape
    tp = lax.axis_size("tp")
    ring = tp // 2
    places = lax.axis_size("seq")
    modes = rates.shape[0]
    tiles = rows // T
    shape = pltpu.HBM
    params = pltpu.CompilerParams(vmem_limit_bytes=24 << 20)

    def turn(a, hop):
        return lax.ppermute(
            a, "tp", [(c * ring + i, c * ring + (i + hop) % ring) for c in range(2) for i in range(ring)]
        )

    def across(a):
        return lax.ppermute(a, "tp", [(i, (i + ring) % tp) for i in range(tp)])

    powers, near, spread_f, spread_b = pl.pallas_call(
        tables_kernel,
        out_shape=(
            shape((T + 2, modes, chans), f32),
            shape((2 * T + 8, chans), f32),
            shape((modes, T, chans), f32),
            shape((modes, T, chans), f32),
        ),
        compiler_params=params,
        name="tables",
    )(rates, residues)
    gain = norm_gain.reshape(tp, 1, chans)
    value_weight, gate_weight, out_weight = far_memory(value_weight, gate_weight, out_weight)

    ups, downs = [], []
    ahead = behind = jnp.stack([hidden, across(hidden)])
    start = ahead
    for _ in range(3):
        ahead, behind = turn(ahead, 1), turn(behind, -1)
        ups.append(ahead)
        downs.append(behind)
    last_up, last_down = turn(ahead[0], 1), turn(behind[1], -1)

    def project(arrays, slots, carried):
        return pl.pallas_call(
            functools.partial(early_kernel, slots, len(arrays), not carried),
            in_specs=[remote] * len(arrays)
            + [whole(gain.shape), remote, remote]
            + [whole(a.shape) for a in carried],
            out_specs=[whole((2, rows, 2 * chans)), whole((rows, chans))],
            out_shape=(shape((2, rows, 2 * chans), f32), shape((rows, chans), f32)),
            scratch_shapes=[
                pltpu.VMEM((len(slots), rows, chans), bf16),
                pltpu.VMEM((len(slots), 2, chans, 2 * chans), bf16),
                pltpu.SemaphoreType.DMA((len(slots), 5)),
            ],
            compiler_params=params,
            cost_estimate=pl.CostEstimate(
                flops=len(slots) * 10 * chans**3, transcendentals=0, bytes_accessed=len(slots) * 10 * chans**2
            ),
            name="project",
        )(*arrays, gain, value_weight, gate_weight, *carried)

    def pair_slots(hops):
        return tuple((n, c, c, hop) for n, hop in enumerate(hops) for c in range(2))

    carried = project([start, ups[0], downs[0], ups[1], downs[1]], pair_slots((0, -1, 1, -2, 2)), ())
    carried = project([ups[2], downs[2]], pair_slots((-3, 3)), far_memory(*carried))

    slots = ((0, None, 0, -4), (1, None, 1, 4))
    send, fore, back, sv, gates, first, last = pl.pallas_call(
        functools.partial(states_kernel, slots, 2),
        in_specs=[remote, remote, whole(gain.shape), remote, remote]
        + [whole(a.shape) for a in carried]
        + [whole(value_taps.shape), whole(powers.shape)],
        out_specs=[
            whole((places, modes, 2 * chans)),
            whole((2, tiles, modes, chans)),
            whole((2, tiles, modes, chans)),
            whole((2, tiles, T, chans)),
            whole((rows, 2 * chans)),
            whole((8, 2 * chans)),
            whole((8, 2 * chans)),
        ],
        out_shape=(
            shape((places, modes, 2 * chans), f32),
            shape((2, tiles, modes, chans), f32),
            shape((2, tiles, modes, chans), f32),
            shape((2, tiles, T, chans), f32),
            shape((rows, 2 * chans), f32),
            shape((8, 2 * chans), f32),
            shape((8, 2 * chans), f32),
        ),
        scratch_shapes=[
            pltpu.VMEM((2, rows, 2 * chans), f32),
            pltpu.VMEM((rows, chans), f32),
            pltpu.VMEM((rows + 16, chans), f32),
            pltpu.VMEM((2, rows, chans), bf16),
            pltpu.VMEM((2, 2, chans, 2 * chans), bf16),
            pltpu.SemaphoreType.DMA((2, 5)),
        ],
        compiler_params=params,
        name="states",
    )(
        last_up, last_down, gain, value_weight, gate_weight, *far_memory(*carried), value_taps,
        *far_memory(powers),
    )

    recv = lax.all_to_all(send, "seq", split_axis=0, concat_axis=0)
    up = [(i, i + 1) for i in range(places - 1)]
    below = lax.ppermute(last, "seq", up)
    above = lax.ppermute(first, "seq", [(b, a) for a, b in up])

    local = pl.pallas_call(
        near_kernel,
        out_shape=shape((2, tiles, T, chans), f32),
        compiler_params=params,
        name="near",
    )(*far_memory(sv, near))

    chunks = ((0, 4), (1, 4))
    square = shape((rows, chans), bf16)
    pair = shape((2, rows, chans), bf16)
    inputs = (
        recv, *far_memory(fore, back, local, gates), above, below, gate_taps, rates,
        *far_memory(spread_f, spread_b),
    )
    z, out_up, out_down = pl.pallas_call(
        functools.partial(gated_kernel, chunks),
        in_specs=[whole(a.shape) for a in inputs] + [remote],
        out_specs=[whole((rows, 2 * chans)), whole((rows, chans)), whole((rows, chans))],
        out_shape=(shape((rows, 2 * chans), bf16), square, square),
        scratch_shapes=[
            pltpu.VMEM((rows + 16, chans), f32),
            pltpu.VMEM((2, tiles, modes, 128), f32),
            pltpu.VMEM((len(chunks), 2, chans, chans), bf16),
            pltpu.SemaphoreType.DMA((len(chunks), 2)),
        ],
        compiler_params=params,
        name="gated",
    )(*inputs, out_weight)
    hops = (3, -3, 2, -2, 1, -1, 0)
    chunks = tuple((c, hop) for hop in hops for c in range(2))
    parts = pl.pallas_call(
        functools.partial(rest_kernel, chunks),
        in_specs=[whole(z.shape), remote],
        out_specs=[whole((2, rows, chans))] * len(hops),
        out_shape=(pair,) * len(hops),
        scratch_shapes=[
            pltpu.VMEM((len(chunks), 2, chans, chans), bf16),
            pltpu.SemaphoreType.DMA((len(chunks), 2)),
        ],
        compiler_params=params,
        cost_estimate=pl.CostEstimate(
            flops=len(chunks) * 6 * chans**3, transcendentals=0, bytes_accessed=len(chunks) * 6 * chans**2
        ),
        name="rest",
    )(*far_memory(z), out_weight)

    up_sum, down_sum = turn(out_up, 1), turn(out_down, -1)
    nothing = jnp.zeros_like(up_sum, f32)
    up_sum = jnp.stack([up_sum.astype(f32), nothing])
    down_sum = jnp.stack([nothing, down_sum.astype(f32)])
    for hop in range(3):
        ups_now = (parts[2 * hop].astype(f32) + up_sum).astype(bf16)
        downs_now = (parts[2 * hop + 1].astype(f32) + down_sum).astype(bf16)
        up_sum, down_sum = turn(ups_now, 1).astype(f32), turn(downs_now, -1).astype(f32)
    total = parts[6].astype(f32) + up_sum + down_sum
    other = across(total[1].astype(bf16))
    return (total[0] + other.astype(f32)).astype(bf16)


def solution(mesh):
    in_specs = (
        P("seq", "tp"),
        P(),
        P(None, "tp"),
        P(None, "tp"),
        P(None, "tp"),
        P(None, "tp"),
        P(None, "tp"),
        P(None, "tp"),
        P("tp", None),
    )
    out_specs = P("seq", "tp")
    return jax.shard_map(body, mesh=mesh, in_specs=in_specs, out_specs=out_specs, check_vma=False)
```

```python
import functools
import jax
import jax.numpy as jnp
from jax import lax
from jax.experimental import pallas as pl
from jax.experimental.pallas import tpu as pltpu
from jax.sharding import PartitionSpec as P

eps = 1e-05
f32 = jnp.float32
bf16 = jnp.bfloat16
T = 16


def tables_kernel(rates_ref, residues_ref, pow_ref, near_ref, fore_ref, back_ref):
    rates = rates_ref[...]
    modes, chans = rates.shape
    strength = residues_ref[...] * jnp.sqrt(rates)
    for k in range(T):
        pow_ref[k] = jnp.exp(-rates * float(k))
    pow_ref[T] = jnp.exp(-rates * float(T))
    pow_ref[T + 1] = jnp.exp(rates)
    steps = lax.broadcasted_iota(jnp.int32, (T, chans), 0).astype(f32)
    total = jnp.zeros((T, chans), f32)
    for m in range(modes):
        rate = rates[m : m + 1, :]
        weight = strength[m : m + 1, :]
        fore = weight * jnp.exp(-rate * (steps + 1.0))
        fore_ref[m] = fore
        back_ref[m] = weight * jnp.exp(-rate * (float(T) - steps))
        total = total + fore
    near_ref[pl.ds(T + 1, T), :] = total
    near_ref[pl.ds(T, 1), :] = jnp.sum(strength, axis=0, keepdims=True)
    for k in range(1, T + 1):
        near_ref[pl.ds(T - k, 1), :] = total[k - 1 : k, :]


def reversal(n):
    i0 = lax.broadcasted_iota(jnp.int32, (n, n), 0)
    i1 = lax.broadcasted_iota(jnp.int32, (n, n), 1)
    return (i0 + i1 == n - 1).astype(f32).astype(bf16)


def shard_at(place, column, hop, tp):
    ring = tp // 2
    return ((place // ring + column) % 2) * ring + (place % ring + hop + ring) % ring


def rows_of(block, size):
    return pl.ds(pl.multiple_of(block * size, size), size)


def accumulate(slots, x_refs, gain_ref, weights, x_buf, w_buf, sems, acc_ref, sq_ref, fresh):
    tp = lax.axis_size("tp")
    place = lax.axis_index("tp")
    rows, chans = x_buf.shape[1:]
    copies = []
    for n, (array, entry, column, hop) in enumerate(slots):
        block = shard_at(place, column, hop, tp)
        source = x_refs[array] if entry is None else x_refs[array].at[entry]
        group = [pltpu.make_async_copy(source, x_buf.at[n], sems.at[n, 0])]
        for w, ref in enumerate(weights):
            lanes = pl.ds(w * chans, chans)
            group.append(
                pltpu.make_async_copy(ref.at[rows_of(block, chans), :], w_buf.at[n, 0, :, lanes], sems.at[n, 1 + w])
            )
            group.append(
                pltpu.make_async_copy(
                    ref.at[rows_of(tp - 1 - block, chans), :], w_buf.at[n, 1, :, lanes], sems.at[n, 3 + w]
                )
            )
        for copy in group:
            copy.start()
        copies.append(group)
    flip = reversal(chans)
    wide = w_buf.shape[3]
    for n, (array, entry, column, hop) in enumerate(slots):
        block = shard_at(place, column, hop, tp)
        for copy in copies[n]:
            copy.wait()
        x = x_buf[n]
        part = x.astype(f32)
        mirrored = jnp.dot(x, flip, preferred_element_type=f32)
        own = (part * gain_ref[block]).astype(bf16)
        far = (mirrored * gain_ref[tp - 1 - block]).astype(bf16)
        first = jnp.dot(own, w_buf[n, 0], preferred_element_type=f32)
        second = jnp.dot(far, w_buf[n, 1], preferred_element_type=f32)
        if fresh and n == 0:
            sq_ref[...] = part * part
            acc_ref[0] = first
            acc_ref[1] = second
        else:
            sq_ref[...] += part * part
            acc_ref[0] += first
            acc_ref[1] += second


def early_kernel(slots, arrays, fresh, *refs):
    x_refs, refs = refs[:arrays], refs[arrays:]
    gain_ref, wv_ref, wg_ref, refs = refs[0], refs[1], refs[2], refs[3:]
    if not fresh:
        acc_in, sq_in, refs = refs[0], refs[1], refs[2:]
    acc_ref, sq_ref, x_buf, w_buf, sems = refs
    if not fresh:
        acc_ref[...] = acc_in[...]
        sq_ref[...] = sq_in[...]
    accumulate(slots, x_refs, gain_ref, (wv_ref, wg_ref), x_buf, w_buf, sems, acc_ref, sq_ref, fresh)


def states_kernel(slots, arrays, *refs):
    x_refs, refs = refs[:arrays], refs[arrays:]
    gain_ref, wv_ref, wg_ref, acc_in, sq_in, vt_ref, pow_ref, refs = *refs[:7], refs[7:]
    send_ref, fore_ref, back_ref, sv_ref, gates_ref, first_ref, last_ref, refs = *refs[:7], refs[7:]
    acc_ref, sq_ref, pad_ref, x_buf, w_buf, sems = refs
    acc_ref[...] = acc_in[...]
    sq_ref[...] = sq_in[...]
    accumulate(slots, x_refs, gain_ref, (wv_ref, wg_ref), x_buf, w_buf, sems, acc_ref, sq_ref, False)
    rows, chans = sq_ref.shape
    place = lax.axis_index("seq")
    places = lax.axis_size("seq")
    mean = jnp.sum(sq_ref[...], axis=1, keepdims=True) * (1.0 / (lax.axis_size("tp") * chans))
    scale = lax.rsqrt(mean + eps)
    low_ok = (place > 0).astype(f32)
    high_ok = (place < places - 1).astype(f32)
    zeros8 = jnp.zeros((8, chans), f32)
    tiles = rows // T
    for s in range(2):
        strand = slice(s * chans, (s + 1) * chans)
        gates = acc_ref[s, :, chans:] * scale
        gates_ref[:, strand] = gates
        first_ref[:, strand] = gates[0:8, :]
        last_ref[:, strand] = gates[rows - 8 : rows, :]
        v = acc_ref[s, :, :chans] * scale
        pad_ref[0:8, :] = zeros8
        pad_ref[8 : 8 + rows, :] = v
        pad_ref[8 + rows : 16 + rows, :] = zeros8
        a, c = (0, 2) if s == 0 else (2, 0)
        ta, tb, tc = vt_ref[a : a + 1, :], vt_ref[1:2, :], vt_ref[c : c + 1, :]
        sv = ta * pad_ref[7 : 7 + rows, :] + tb * v + tc * pad_ref[9 : 9 + rows, :]
        sv_ref[s] = sv.reshape(tiles, T, chans)
        all_low = tc * v[0:1, :] * low_ok
        all_high = ta * v[rows - 1 : rows, :] * high_ok
        for g in range(chans // 128):
            lanes = slice(g * 128, (g + 1) * 128)
            low, high = all_low[:, lanes], all_high[:, lanes]
            jump = pow_ref[T, :, lanes]
            inverse = pow_ref[T + 1, :, lanes]
            fold = jnp.zeros((tiles, 16, 128), f32)
            for j in range(T):
                fold = fold + pow_ref[T - 1 - j, :, lanes][None] * sv_ref[s, :, j : j + 1, lanes]
            state = jnp.broadcast_to(low, (16, 128))
            for n in range(tiles):
                fore_ref[s, n, :, lanes] = state
                state = jump * state + fold[n]
            ahead = state + inverse * high
            fold = jnp.zeros((tiles, 16, 128), f32)
            for j in range(T):
                fold = fold + pow_ref[j, :, lanes][None] * sv_ref[s, :, j : j + 1, lanes]
            state = jnp.broadcast_to(high, (16, 128))
            for n in reversed(range(tiles)):
                back_ref[s, n, :, lanes] = state
                state = jump * state + fold[n]
            behind = state + inverse * low
            wide = slice(s * chans + g * 128, s * chans + (g + 1) * 128)
            for i in range(places):
                send_ref[i, :, wide] = jnp.where(i > place, ahead, behind)


def near_kernel(sv_ref, near_ref, local_ref):
    tiles = sv_ref.shape[1]
    chans = sv_ref.shape[3]
    for s in range(2):
        for g in range(chans // 128):
            lanes = slice(g * 128, (g + 1) * 128)
            inner = jnp.zeros((tiles, T, 128), f32)
            for j in range(T):
                inner = inner + near_ref[T - j : 2 * T - j, lanes][None] * sv_ref[s, :, j : j + 1, lanes]
            local_ref[s, :, :, lanes] = inner


def fetch_columns(chunks, wo_ref, w_buf, sems):
    tp = lax.axis_size("tp")
    place = lax.axis_index("tp")
    chans = w_buf.shape[2]
    copies = []
    for n, (column, hop) in enumerate(chunks):
        block = shard_at(place, column, hop, tp)
        pair = (
            pltpu.make_async_copy(wo_ref.at[:, rows_of(block, chans)], w_buf.at[n, 0], sems.at[n, 0]),
            pltpu.make_async_copy(wo_ref.at[:, rows_of(tp - 1 - block, chans)], w_buf.at[n, 1], sems.at[n, 1]),
        )
        for copy in pair:
            copy.start()
        copies.append(pair)
    return copies


def partial_chunk(n, copies, z_ref, w_buf, flip):
    chans = w_buf.shape[2]
    for copy in copies[n]:
        copy.wait()
    far = jnp.dot(w_buf[n, 1], flip, preferred_element_type=f32).astype(bf16)
    out = jnp.dot(z_ref[:, :chans], w_buf[n, 0], preferred_element_type=f32)
    return out + jnp.dot(z_ref[:, chans:], far, preferred_element_type=f32)


def gated_kernel(
    chunks, recv_ref, fore_ref, back_ref, local_ref, gates_ref, above_ref, below_ref, gt_ref, rates_ref,
    spread_f_ref, spread_b_ref, wo_ref, z_ref, *refs,
):
    outs, (pad_ref, st_ref, w_buf, sems) = refs[: len(chunks)], refs[len(chunks) :]
    rows = gates_ref.shape[0]
    chans = gates_ref.shape[1] // 2
    tiles = rows // T
    place = lax.axis_index("seq")
    places = lax.axis_size("seq")
    copies = fetch_columns(chunks, wo_ref, w_buf, sems)
    for s in range(2):
        wide = slice(s * chans, (s + 1) * chans)
        g = gates_ref[:, wide]
        pad_ref[0:8, :] = below_ref[:, wide]
        pad_ref[8 : 8 + rows, :] = g
        pad_ref[8 + rows : 16 + rows, :] = above_ref[:, wide]
        a, c = (0, 2) if s == 0 else (2, 0)
        ta, tb, tc = gt_ref[a : a + 1, :], gt_ref[1:2, :], gt_ref[c : c + 1, :]
        sg = ta * pad_ref[7 : 7 + rows, :] + tb * g + tc * pad_ref[9 : 9 + rows, :]
        for g2 in range(chans // 128):
            lanes = slice(g2 * 128, (g2 + 1) * 128)
            wide = slice(s * chans + g2 * 128, s * chans + (g2 + 1) * 128)
            rates = rates_ref[:, lanes]
            hop = jnp.exp(-rates * float(rows))
            jump = jnp.exp(-rates * float(T))
            carry_f = jnp.zeros((16, 128), f32)
            carry_b = jnp.zeros((16, 128), f32)
            for j in range(places):
                r = places - 1 - j
                carry_f = jnp.where(j < place, carry_f * hop + recv_ref[j, :, wide], carry_f)
                carry_b = jnp.where(r > place, carry_b * hop + recv_ref[r, :, wide], carry_b)
            for n in range(tiles):
                m = tiles - 1 - n
                st_ref[0, n] = fore_ref[s, n, :, lanes] + carry_f
                st_ref[1, m] = back_ref[s, m, :, lanes] + carry_b
                carry_f = carry_f * jump
                carry_b = carry_b * jump
            conv = local_ref[s, :, :, lanes]
            for m in range(16):
                conv = conv + spread_f_ref[m, :, lanes][None] * st_ref[0, :, m : m + 1, :]
            for m in range(16):
                conv = conv + spread_b_ref[m, :, lanes][None] * st_ref[1, :, m : m + 1, :]
            z_ref[:, wide] = (sg[:, lanes] * conv.reshape(rows, 128)).astype(bf16)
    flip = reversal(chans)
    for n, ref in enumerate(outs):
        ref[...] = partial_chunk(n, copies, z_ref, w_buf, flip).astype(bf16)


def rest_kernel(chunks, z_ref, wo_ref, *refs):
    outs, (w_buf, sems) = refs[:-2], refs[-2:]
    copies = fetch_columns(chunks, wo_ref, w_buf, sems)
    flip = reversal(w_buf.shape[2])
    for n in range(len(chunks)):
        outs[n // 2][n % 2] = partial_chunk(n, copies, z_ref, w_buf, flip).astype(bf16)


def far_memory(*arrays):
    return [pltpu.with_memory_space_constraint(a, pltpu.HBM) for a in arrays]


def whole(shape):
    return pl.BlockSpec(shape, lambda *_: (0,) * len(shape))


remote = pl.BlockSpec(memory_space=pl.ANY)


def body(
    hidden, norm_gain, value_weight, gate_weight, value_taps, gate_taps, rates, residues, out_weight
):
    rows, chans = hidden.shape
    tp = lax.axis_size("tp")
    ring = tp // 2
    places = lax.axis_size("seq")
    modes = rates.shape[0]
    tiles = rows // T
    shape = pltpu.HBM
    params = pltpu.CompilerParams(vmem_limit_bytes=24 << 20)

    def turn(a, hop):
        return lax.ppermute(
            a, "tp", [(c * ring + i, c * ring + (i + hop) % ring) for c in range(2) for i in range(ring)]
        )

    def across(a):
        return lax.ppermute(a, "tp", [(i, (i + ring) % tp) for i in range(tp)])

    rates, residues = far_memory(rates, residues)
    powers, near, spread_f, spread_b = pl.pallas_call(
        tables_kernel,
        out_shape=(
            shape((T + 2, modes, chans), f32),
            shape((2 * T + 8, chans), f32),
            shape((modes, T, chans), f32),
            shape((modes, T, chans), f32),
        ),
        compiler_params=params,
        name="tables",
    )(rates, residues)
    gain = norm_gain.reshape(tp, 1, chans)
    value_weight, gate_weight, out_weight = far_memory(value_weight, gate_weight, out_weight)
    gain, value_taps, gate_taps = far_memory(gain, value_taps, gate_taps)

    def project(arrays, slots, carried):
        return pl.pallas_call(
            functools.partial(early_kernel, slots, len(arrays), not carried),
            in_specs=[remote] * len(arrays)
            + [whole(gain.shape), remote, remote]
            + [whole(a.shape) for a in carried],
            out_specs=[whole((2, rows, 2 * chans)), whole((rows, chans))],
            out_shape=(shape((2, rows, 2 * chans), f32), shape((rows, chans), f32)),
            scratch_shapes=[
                pltpu.VMEM((len(slots), rows, chans), bf16),
                pltpu.VMEM((len(slots), 2, chans, 2 * chans), bf16),
                pltpu.SemaphoreType.DMA((len(slots), 5)),
            ],
            compiler_params=params,
            cost_estimate=pl.CostEstimate(
                flops=len(slots) * 10 * chans**3, transcendentals=0, bytes_accessed=len(slots) * 10 * chans**2
            ),
            name="project",
        )(*arrays, gain, value_weight, gate_weight, *carried)

    def pair_slots(hops):
        return tuple((n, c, c, hop) for n, hop in enumerate(hops) for c in range(2))

    start = jnp.stack([hidden, across(hidden)])
    up1, down1 = turn(start, 1), turn(start, -1)
    up1, down1, powers, near, spread_f, spread_b = lax.optimization_barrier(
        (up1, down1, powers, near, spread_f, spread_b)
    )
    up2, down2 = turn(up1, 1), turn(down1, -1)
    up3, down3 = turn(up2, 1), turn(down2, -1)
    carried = project([start, up1, down1, up2, down2], pair_slots((0, -1, 1, -2, 2)), ())
    up3, down3, carried = lax.optimization_barrier((up3, down3, carried))
    last_up, last_down = turn(up3[0], 1), turn(down3[1], -1)
    carried = project([up3, down3], pair_slots((-3, 3)), far_memory(*carried))

    slots = ((0, None, 0, -4), (1, None, 1, 4))
    send, fore, back, sv, gates, first, last = pl.pallas_call(
        functools.partial(states_kernel, slots, 2),
        in_specs=[remote, remote, whole(gain.shape), remote, remote]
        + [whole(a.shape) for a in carried]
        + [whole(value_taps.shape), whole(powers.shape)],
        out_specs=[
            whole((places, modes, 2 * chans)),
            whole((2, tiles, modes, chans)),
            whole((2, tiles, modes, chans)),
            whole((2, tiles, T, chans)),
            whole((rows, 2 * chans)),
            whole((8, 2 * chans)),
            whole((8, 2 * chans)),
        ],
        out_shape=(
            shape((places, modes, 2 * chans), f32),
            shape((2, tiles, modes, chans), f32),
            shape((2, tiles, modes, chans), f32),
            shape((2, tiles, T, chans), f32),
            shape((rows, 2 * chans), f32),
            shape((8, 2 * chans), f32),
            shape((8, 2 * chans), f32),
        ),
        scratch_shapes=[
            pltpu.VMEM((2, rows, 2 * chans), f32),
            pltpu.VMEM((rows, chans), f32),
            pltpu.VMEM((rows + 16, chans), f32),
            pltpu.VMEM((2, rows, chans), bf16),
            pltpu.VMEM((2, 2, chans, 2 * chans), bf16),
            pltpu.SemaphoreType.DMA((2, 5)),
        ],
        compiler_params=params,
        name="states",
    )(
        last_up, last_down, gain, value_weight, gate_weight, *far_memory(*carried), value_taps,
        *far_memory(powers),
    )

    recv = lax.all_to_all(send, "seq", split_axis=0, concat_axis=0)
    up = [(i, i + 1) for i in range(places - 1)]
    below = lax.ppermute(last, "seq", up)
    above = lax.ppermute(first, "seq", [(b, a) for a, b in up])

    local = pl.pallas_call(
        near_kernel,
        out_shape=shape((2, tiles, T, chans), f32),
        compiler_params=params,
        name="near",
    )(*far_memory(sv, near))

    chunks = ((0, 4), (1, 4))
    square = shape((rows, chans), bf16)
    pair = shape((2, rows, chans), bf16)
    inputs = (
        recv, *far_memory(fore, back, local, gates), above, below, gate_taps, rates,
        *far_memory(spread_f, spread_b),
    )
    z, out_up, out_down = pl.pallas_call(
        functools.partial(gated_kernel, chunks),
        in_specs=[whole(a.shape) for a in inputs] + [remote],
        out_specs=[whole((rows, 2 * chans)), whole((rows, chans)), whole((rows, chans))],
        out_shape=(shape((rows, 2 * chans), bf16), square, square),
        scratch_shapes=[
            pltpu.VMEM((rows + 16, chans), f32),
            pltpu.VMEM((2, tiles, modes, 128), f32),
            pltpu.VMEM((len(chunks), 2, chans, chans), bf16),
            pltpu.SemaphoreType.DMA((len(chunks), 2)),
        ],
        compiler_params=params,
        name="gated",
    )(*inputs, out_weight)

    def rest(z, hops):
        chunks = tuple((c, hop) for hop in hops for c in range(2))
        return pl.pallas_call(
            functools.partial(rest_kernel, chunks),
            in_specs=[whole(z.shape), remote],
            out_specs=[whole((2, rows, chans))] * len(hops),
            out_shape=(pair,) * len(hops),
            scratch_shapes=[
                pltpu.VMEM((len(chunks), 2, chans, chans), bf16),
                pltpu.SemaphoreType.DMA((len(chunks), 2)),
            ],
            compiler_params=params,
            cost_estimate=pl.CostEstimate(
                flops=len(chunks) * 6 * chans**3, transcendentals=0, bytes_accessed=len(chunks) * 6 * chans**2
            ),
            name="rest",
        )(*far_memory(z), out_weight)

    up_sum, down_sum = turn(out_up, 1), turn(out_down, -1)
    nothing = jnp.zeros_like(up_sum, f32)
    up_sum = jnp.stack([up_sum.astype(f32), nothing])
    down_sum = jnp.stack([nothing, down_sum.astype(f32)])
    parts = rest(z, (3, -3))
    for hop in (2, 1, 0):
        ups_now = (parts[0].astype(f32) + up_sum).astype(bf16)
        downs_now = (parts[1].astype(f32) + down_sum).astype(bf16)
        ups_now, downs_now, z = lax.optimization_barrier((ups_now, downs_now, z))
        up_sum, down_sum = turn(ups_now, 1).astype(f32), turn(downs_now, -1).astype(f32)
        parts = rest(z, (hop, -hop) if hop else (0,))
    total = parts[0].astype(f32) + up_sum + down_sum
    other = across(total[1].astype(bf16))
    return (total[0] + other.astype(f32)).astype(bf16)


def solution(mesh):
    in_specs = (
        P("seq", "tp"),
        P(),
        P(None, "tp"),
        P(None, "tp"),
        P(None, "tp"),
        P(None, "tp"),
        P(None, "tp"),
        P(None, "tp"),
        P("tp", None),
    )
    out_specs = P("seq", "tp")
    return jax.shard_map(body, mesh=mesh, in_specs=in_specs, out_specs=out_specs, check_vma=False)
```

```python
import functools
import jax
import jax.numpy as jnp
from jax import lax
from jax.experimental import pallas as pl
from jax.experimental.pallas import tpu as pltpu
from jax.sharding import PartitionSpec as P

eps = 1e-05
f32 = jnp.float32
bf16 = jnp.bfloat16
T = 16


def tables_kernel(rates_ref, residues_ref, pow_ref, near_ref, fore_ref, back_ref):
    rates = rates_ref[...]
    modes, chans = rates.shape
    strength = residues_ref[...] * jnp.sqrt(rates)
    for k in range(T):
        pow_ref[k] = jnp.exp(-rates * float(k))
    pow_ref[T] = jnp.exp(-rates * float(T))
    pow_ref[T + 1] = jnp.exp(rates)
    steps = lax.broadcasted_iota(jnp.int32, (T, chans), 0).astype(f32)
    total = jnp.zeros((T, chans), f32)
    for m in range(modes):
        rate = rates[m : m + 1, :]
        weight = strength[m : m + 1, :]
        fore = weight * jnp.exp(-rate * (steps + 1.0))
        fore_ref[m] = fore
        back_ref[m] = weight * jnp.exp(-rate * (float(T) - steps))
        total = total + fore
    near_ref[pl.ds(T + 1, T), :] = total
    near_ref[pl.ds(T, 1), :] = jnp.sum(strength, axis=0, keepdims=True)
    for k in range(1, T + 1):
        near_ref[pl.ds(T - k, 1), :] = total[k - 1 : k, :]


def reversal(n):
    i0 = lax.broadcasted_iota(jnp.int32, (n, n), 0)
    i1 = lax.broadcasted_iota(jnp.int32, (n, n), 1)
    return (i0 + i1 == n - 1).astype(f32).astype(bf16)


def shard_at(place, column, hop, tp):
    ring = tp // 2
    return ((place // ring + column) % 2) * ring + (place % ring + hop + ring) % ring


def rows_of(block, size):
    return pl.ds(pl.multiple_of(block * size, size), size)


def accumulate(slots, x_refs, gain_ref, weights, x_buf, w_buf, sems, acc_ref, sq_ref, carried=(), sinks=()):
    tp = lax.axis_size("tp")
    place = lax.axis_index("tp")
    rows, chans = x_buf.shape[1:]
    last = len(slots)
    copies = []
    for n, (array, entry, column, hop) in enumerate(slots):
        block = shard_at(place, column, hop, tp)
        source = x_refs[array] if entry is None else x_refs[array].at[entry]
        group = [pltpu.make_async_copy(source, x_buf.at[n], sems.at[n, 0])]
        for w, ref in enumerate(weights):
            lanes = pl.ds(w * chans, chans)
            group.append(
                pltpu.make_async_copy(ref.at[rows_of(block, chans), :], w_buf.at[n, 0, :, lanes], sems.at[n, 1 + w])
            )
            group.append(
                pltpu.make_async_copy(
                    ref.at[rows_of(tp - 1 - block, chans), :], w_buf.at[n, 1, :, lanes], sems.at[n, 3 + w]
                )
            )
        for copy in group:
            copy.start()
        copies.append(group)
        if n == 0 and carried:
            acc_in, sq_in = carried
            before = [
                pltpu.make_async_copy(acc_in.at[0], acc_ref.at[0], sems.at[last, 0]),
                pltpu.make_async_copy(acc_in.at[1], acc_ref.at[1], sems.at[last, 1]),
                pltpu.make_async_copy(sq_in, sq_ref, sems.at[last, 2]),
            ]
            for copy in before:
                copy.start()
    flip = reversal(chans)
    after = []

    def leave(index, source, sink, ready):
        if sinks and ready:
            copy = pltpu.make_async_copy(source, sink, sems.at[last + 1, index])
            copy.start()
            after.append(copy)

    for n, (array, entry, column, hop) in enumerate(slots):
        block = shard_at(place, column, hop, tp)
        for copy in copies[n]:
            copy.wait()
        x = x_buf[n]
        part = x.astype(f32)
        square = part * part
        square = sum(square[:, i : i + 128] for i in range(0, chans, 128))
        mirrored = jnp.dot(x, flip, preferred_element_type=f32)
        own = (part * gain_ref[block]).astype(bf16)
        far = (mirrored * gain_ref[tp - 1 - block]).astype(bf16)
        first = jnp.dot(own, w_buf[n, 0], preferred_element_type=f32)
        if n == 0 and carried:
            for copy in before:
                copy.wait()
        fresh = n == 0 and not carried
        done = n == last - 1
        acc_ref[0] = first if fresh else acc_ref[0] + first
        sq_ref[...] = square if fresh else sq_ref[...] + square
        if sinks:
            leave(0, acc_ref.at[0], sinks[0].at[0], done)
            leave(2, sq_ref, sinks[1], done)
        second = jnp.dot(far, w_buf[n, 1], preferred_element_type=f32)
        acc_ref[1] = second if fresh else acc_ref[1] + second
        if sinks:
            leave(1, acc_ref.at[1], sinks[0].at[1], done)
    for copy in after:
        copy.wait()


def early_kernel(slots, arrays, more, *refs):
    x_refs, refs = refs[:arrays], refs[arrays:]
    gain_ref, wv_ref, wg_ref, refs = refs[0], refs[1], refs[2], refs[3:]
    carried, sinks, refs = refs[:more], refs[more : more + 2], refs[more + 2 :]
    acc_ref, sq_ref, x_buf, w_buf, sems = refs
    accumulate(slots, x_refs, gain_ref, (wv_ref, wg_ref), x_buf, w_buf, sems, acc_ref, sq_ref, carried, sinks)


def states_kernel(slots, arrays, *refs):
    x_refs, refs = refs[:arrays], refs[arrays:]
    gain_ref, wv_ref, wg_ref, acc_in, sq_in, vt_ref, pow_ref, refs = *refs[:7], refs[7:]
    send_ref, sv_ref, gates_ref, edge_ref, refs = *refs[:4], refs[4:]
    acc_ref, sq_ref, pad_ref, x_buf, w_buf, sems = refs
    accumulate(
        slots, x_refs, gain_ref, (wv_ref, wg_ref), x_buf, w_buf, sems, acc_ref, sq_ref, (acc_in, sq_in)
    )
    rows, chans = x_buf.shape[1:]
    place = lax.axis_index("seq")
    places = lax.axis_size("seq")
    mean = jnp.sum(sq_ref[...], axis=1, keepdims=True) * (1.0 / (lax.axis_size("tp") * chans))
    scale = lax.rsqrt(mean + eps)
    low_ok = (place > 0).astype(f32)
    high_ok = (place < places - 1).astype(f32)
    zeros8 = jnp.zeros((8, chans), f32)
    tiles = rows // T
    for s in range(2):
        strand = slice(s * chans, (s + 1) * chans)
        gates = acc_ref[s, :, chans:] * scale
        gates_ref[:, strand] = gates
        for g in range(chans // 128):
            row = s * (chans // 128) + g
            first = gates[0:1, g * 128 : (g + 1) * 128]
            last = gates[rows - 1 : rows, g * 128 : (g + 1) * 128]
            for i in range(places):
                send_ref[i, row : row + 1, 2 * chans :] = jnp.where(i > place, last, first)
        v = acc_ref[s, :, :chans] * scale
        pad_ref[0:8, :] = zeros8
        pad_ref[8 : 8 + rows, :] = v
        pad_ref[8 + rows : 16 + rows, :] = zeros8
        a, c = (0, 2) if s == 0 else (2, 0)
        ta, tb, tc = vt_ref[a : a + 1, :], vt_ref[1:2, :], vt_ref[c : c + 1, :]
        sv = ta * pad_ref[7 : 7 + rows, :] + tb * v + tc * pad_ref[9 : 9 + rows, :]
        sv_ref[s] = sv.reshape(tiles, T, chans)
        all_low = tc * v[0:1, :] * low_ok
        all_high = ta * v[rows - 1 : rows, :] * high_ok
        edge_ref[s, 0] = jnp.broadcast_to(all_low, (8, chans))
        edge_ref[s, 1] = jnp.broadcast_to(all_high, (8, chans))
        for g in range(chans // 128):
            lanes = slice(g * 128, (g + 1) * 128)
            low, high = all_low[:, lanes], all_high[:, lanes]
            jump = pow_ref[T, :, lanes]
            inverse = pow_ref[T + 1, :, lanes]
            fold = jnp.zeros((tiles, 16, 128), f32)
            for j in range(T):
                fold = fold + pow_ref[T - 1 - j, :, lanes][None] * sv_ref[s, :, j : j + 1, lanes]
            state = jnp.broadcast_to(low, (16, 128))
            for n in range(tiles):
                state = jump * state + fold[n]
            ahead = state + inverse * high
            fold = jnp.zeros((tiles, 16, 128), f32)
            for j in range(T):
                fold = fold + pow_ref[j, :, lanes][None] * sv_ref[s, :, j : j + 1, lanes]
            state = jnp.broadcast_to(high, (16, 128))
            for n in reversed(range(tiles)):
                state = jump * state + fold[n]
            behind = state + inverse * low
            wide = slice(s * chans + g * 128, s * chans + (g + 1) * 128)
            for i in range(places):
                send_ref[i, :, wide] = jnp.where(i > place, ahead, behind)


def spread(conv, spread_f_ref, spread_b_ref, st_ref, lanes):
    for m in range(16):
        conv = conv + spread_f_ref[m, :, lanes][None] * st_ref[0, :, m : m + 1, :]
    for m in range(16):
        conv = conv + spread_b_ref[m, :, lanes][None] * st_ref[1, :, m : m + 1, :]
    return conv


def local_kernel(sv_ref, edge_ref, pow_ref, near_ref, spread_f_ref, spread_b_ref, local_ref, st_ref):
    tiles = sv_ref.shape[1]
    chans = sv_ref.shape[3]
    for s in range(2):
        for g in range(chans // 128):
            lanes = slice(g * 128, (g + 1) * 128)
            jump = pow_ref[T, :, lanes]
            fold = jnp.zeros((tiles, 16, 128), f32)
            for j in range(T):
                fold = fold + pow_ref[T - 1 - j, :, lanes][None] * sv_ref[s, :, j : j + 1, lanes]
            state = jnp.broadcast_to(edge_ref[s, 0, 0:1, lanes], (16, 128))
            for n in range(tiles):
                st_ref[0, n] = state
                state = jump * state + fold[n]
            fold = jnp.zeros((tiles, 16, 128), f32)
            for j in range(T):
                fold = fold + pow_ref[j, :, lanes][None] * sv_ref[s, :, j : j + 1, lanes]
            state = jnp.broadcast_to(edge_ref[s, 1, 0:1, lanes], (16, 128))
            for n in reversed(range(tiles)):
                st_ref[1, n] = state
                state = jump * state + fold[n]
            conv = jnp.zeros((tiles, T, 128), f32)
            for j in range(T):
                conv = conv + near_ref[T - j : 2 * T - j, lanes][None] * sv_ref[s, :, j : j + 1, lanes]
            local_ref[s, :, :, lanes] = spread(conv, spread_f_ref, spread_b_ref, st_ref, lanes)


def fetch_columns(chunks, wo_ref, w_buf, sems):
    tp = lax.axis_size("tp")
    place = lax.axis_index("tp")
    chans = w_buf.shape[2]
    copies = []
    for n, (column, hop) in enumerate(chunks):
        block = shard_at(place, column, hop, tp)
        pair = (
            pltpu.make_async_copy(wo_ref.at[:, rows_of(block, chans)], w_buf.at[n, 0], sems.at[n, 0]),
            pltpu.make_async_copy(wo_ref.at[:, rows_of(tp - 1 - block, chans)], w_buf.at[n, 1], sems.at[n, 1]),
        )
        for copy in pair:
            copy.start()
        copies.append(pair)
    return copies


def partial_chunk(n, copies, z_ref, w_buf, flip):
    chans = w_buf.shape[2]
    for copy in copies[n]:
        copy.wait()
    far = jnp.dot(w_buf[n, 1], flip, preferred_element_type=f32).astype(bf16)
    out = jnp.dot(z_ref[:, :chans], w_buf[n, 0], preferred_element_type=f32)
    return out + jnp.dot(z_ref[:, chans:], far, preferred_element_type=f32)


def gated_kernel(
    chunks, recv_ref, local_ref, gates_ref, gt_ref, rates_ref,
    spread_f_ref, spread_b_ref, wo_ref, z_ref, *refs,
):
    outs, (pad_ref, st_ref, w_buf, sems) = refs[: len(chunks)], refs[len(chunks) :]
    rows = gates_ref.shape[0]
    chans = gates_ref.shape[1] // 2
    tiles = rows // T
    place = lax.axis_index("seq")
    places = lax.axis_size("seq")
    low_ok = (place > 0).astype(f32)
    high_ok = (place < places - 1).astype(f32)
    below = jnp.maximum(place - 1, 0)
    above = jnp.minimum(place + 1, places - 1)
    copies = fetch_columns(chunks, wo_ref, w_buf, sems)
    for s in range(2):
        wide = slice(s * chans, (s + 1) * chans)
        g = gates_ref[:, wide]
        pad_ref[8 : 8 + rows, :] = g
        for g2 in range(chans // 128):
            row = s * (chans // 128) + g2
            lanes = slice(g2 * 128, (g2 + 1) * 128)
            pad_ref[7:8, lanes] = recv_ref[below, row : row + 1, 2 * chans :] * low_ok
            pad_ref[8 + rows : 9 + rows, lanes] = recv_ref[above, row : row + 1, 2 * chans :] * high_ok
        a, c = (0, 2) if s == 0 else (2, 0)
        ta, tb, tc = gt_ref[a : a + 1, :], gt_ref[1:2, :], gt_ref[c : c + 1, :]
        sg = ta * pad_ref[7 : 7 + rows, :] + tb * g + tc * pad_ref[9 : 9 + rows, :]
        for g2 in range(chans // 128):
            lanes = slice(g2 * 128, (g2 + 1) * 128)
            wide = slice(s * chans + g2 * 128, s * chans + (g2 + 1) * 128)
            rates = rates_ref[:, lanes]
            hop = jnp.exp(-rates * float(rows))
            jump = jnp.exp(-rates * float(T))
            carry_f = jnp.zeros((16, 128), f32)
            carry_b = jnp.zeros((16, 128), f32)
            for j in range(places):
                r = places - 1 - j
                carry_f = jnp.where(j < place, carry_f * hop + recv_ref[j, :, wide], carry_f)
                carry_b = jnp.where(r > place, carry_b * hop + recv_ref[r, :, wide], carry_b)
            for n in range(tiles):
                m = tiles - 1 - n
                st_ref[0, n] = carry_f
                st_ref[1, m] = carry_b
                carry_f = carry_f * jump
                carry_b = carry_b * jump
            conv = spread(local_ref[s, :, :, lanes], spread_f_ref, spread_b_ref, st_ref, lanes)
            z_ref[:, wide] = (sg[:, lanes] * conv.reshape(rows, 128)).astype(bf16)
    flip = reversal(chans)
    for n, ref in enumerate(outs):
        ref[...] = partial_chunk(n, copies, z_ref, w_buf, flip).astype(bf16)


def rest_kernel(chunks, z_ref, wo_ref, *refs):
    outs, (w_buf, sems) = refs[:-2], refs[-2:]
    copies = fetch_columns(chunks, wo_ref, w_buf, sems)
    flip = reversal(w_buf.shape[2])
    for n in range(len(chunks)):
        outs[n // 2][n % 2] = partial_chunk(n, copies, z_ref, w_buf, flip).astype(bf16)


def far_memory(*arrays):
    return [pltpu.with_memory_space_constraint(a, pltpu.HBM) for a in arrays]


def whole(shape):
    return pl.BlockSpec(shape, lambda *_: (0,) * len(shape))


remote = pl.BlockSpec(memory_space=pl.ANY)


def body(
    hidden, norm_gain, value_weight, gate_weight, value_taps, gate_taps, rates, residues, out_weight
):
    rows, chans = hidden.shape
    tp = lax.axis_size("tp")
    ring = tp // 2
    places = lax.axis_size("seq")
    modes = rates.shape[0]
    tiles = rows // T
    shape = pltpu.HBM
    params = pltpu.CompilerParams(vmem_limit_bytes=24 << 20)

    def turn(a, hop):
        return lax.ppermute(
            a, "tp", [(c * ring + i, c * ring + (i + hop) % ring) for c in range(2) for i in range(ring)]
        )

    def across(a):
        return lax.ppermute(a, "tp", [(i, (i + ring) % tp) for i in range(tp)])

    rates, residues = far_memory(rates, residues)
    powers, near, spread_f, spread_b = pl.pallas_call(
        tables_kernel,
        out_shape=(
            shape((T + 2, modes, chans), f32),
            shape((2 * T + 8, chans), f32),
            shape((modes, T, chans), f32),
            shape((modes, T, chans), f32),
        ),
        compiler_params=params,
        name="tables",
    )(rates, residues)
    gain = norm_gain.reshape(tp, 1, chans)
    value_weight, gate_weight, out_weight = far_memory(value_weight, gate_weight, out_weight)
    gain, value_taps, gate_taps = far_memory(gain, value_taps, gate_taps)

    def project(arrays, slots, carried):
        return pl.pallas_call(
            functools.partial(early_kernel, slots, len(arrays), len(carried)),
            in_specs=[remote] * len(arrays) + [whole(gain.shape), remote, remote] + [remote] * len(carried),
            out_specs=[remote, remote],
            out_shape=(shape((2, rows, 2 * chans), f32), shape((rows, 128), f32)),
            scratch_shapes=[
                pltpu.VMEM((2, rows, 2 * chans), f32),
                pltpu.VMEM((rows, 128), f32),
                pltpu.VMEM((len(slots), rows, chans), bf16),
                pltpu.VMEM((len(slots), 2, chans, 2 * chans), bf16),
                pltpu.SemaphoreType.DMA((len(slots) + 2, 5)),
            ],
            compiler_params=params,
            cost_estimate=pl.CostEstimate(
                flops=len(slots) * 10 * chans**3, transcendentals=0, bytes_accessed=len(slots) * 10 * chans**2
            ),
            name="project",
        )(*arrays, gain, value_weight, gate_weight, *carried)

    def pair_slots(hops):
        return tuple((n, c, c, hop) for n, hop in enumerate(hops) for c in range(2))

    start = jnp.stack([hidden, across(hidden)])
    up1, down1 = turn(start, 1), turn(start, -1)
    up1, powers, near, spread_f, spread_b = lax.optimization_barrier((up1, powers, near, spread_f, spread_b))
    up2, down2 = turn(up1, 1), turn(down1, -1)
    carried = project([start, up1, down1], pair_slots((0, -1, 1)), ())
    up2, carried = lax.optimization_barrier((up2, carried))
    up3, down3 = turn(up2, 1), turn(down2, -1)
    carried = project([up2, down2], pair_slots((-2, 2)), far_memory(*carried))
    up3, carried = lax.optimization_barrier((up3, carried))
    last_up, last_down = turn(up3[0], 1), turn(down3[1], -1)
    carried = project([up3, down3], pair_slots((-3, 3)), far_memory(*carried))

    slots = ((0, None, 0, -4), (1, None, 1, 4))
    send, sv, gates, edge = pl.pallas_call(
        functools.partial(states_kernel, slots, 2),
        in_specs=[remote, remote, whole(gain.shape), remote, remote, remote, remote]
        + [whole(value_taps.shape), whole(powers.shape)],
        out_specs=[
            whole((places, modes, 2 * chans + 128)),
            whole((2, tiles, T, chans)),
            whole((rows, 2 * chans)),
            whole((2, 2, 8, chans)),
        ],
        out_shape=(
            shape((places, modes, 2 * chans + 128), f32),
            shape((2, tiles, T, chans), f32),
            shape((rows, 2 * chans), f32),
            shape((2, 2, 8, chans), f32),
        ),
        scratch_shapes=[
            pltpu.VMEM((2, rows, 2 * chans), f32),
            pltpu.VMEM((rows, 128), f32),
            pltpu.VMEM((rows + 16, chans), f32),
            pltpu.VMEM((2, rows, chans), bf16),
            pltpu.VMEM((2, 2, chans, 2 * chans), bf16),
            pltpu.SemaphoreType.DMA((4, 5)),
        ],
        compiler_params=params,
        name="states",
    )(
        last_up, last_down, gain, value_weight, gate_weight, *far_memory(*carried), value_taps,
        *far_memory(powers),
    )

    recv = lax.all_to_all(send, "seq", split_axis=0, concat_axis=0)
    local = pl.pallas_call(
        local_kernel,
        out_shape=shape((2, tiles, T, chans), f32),
        scratch_shapes=[pltpu.VMEM((2, tiles, modes, 128), f32)],
        compiler_params=params,
        name="local",
    )(*far_memory(sv, edge, powers, near, spread_f, spread_b))

    chunks = ((0, 4), (1, 4))
    square = shape((rows, chans), bf16)
    pair = shape((2, rows, chans), bf16)
    inputs = (
        recv, *far_memory(local, gates), gate_taps, rates,
        *far_memory(spread_f, spread_b),
    )
    z, out_up, out_down = pl.pallas_call(
        functools.partial(gated_kernel, chunks),
        in_specs=[whole(a.shape) for a in inputs] + [remote],
        out_specs=[whole((rows, 2 * chans)), whole((rows, chans)), whole((rows, chans))],
        out_shape=(shape((rows, 2 * chans), bf16), square, square),
        scratch_shapes=[
            pltpu.VMEM((rows + 16, chans), f32),
            pltpu.VMEM((2, tiles, modes, 128), f32),
            pltpu.VMEM((len(chunks), 2, chans, chans), bf16),
            pltpu.SemaphoreType.DMA((len(chunks), 2)),
        ],
        compiler_params=params,
        name="gated",
    )(*inputs, out_weight)

    def rest(z, hops):
        chunks = tuple((c, hop) for hop in hops for c in range(2))
        return pl.pallas_call(
            functools.partial(rest_kernel, chunks),
            in_specs=[whole(z.shape), remote],
            out_specs=[whole((2, rows, chans))] * len(hops),
            out_shape=(pair,) * len(hops),
            scratch_shapes=[
                pltpu.VMEM((len(chunks), 2, chans, chans), bf16),
                pltpu.SemaphoreType.DMA((len(chunks), 2)),
            ],
            compiler_params=params,
            cost_estimate=pl.CostEstimate(
                flops=len(chunks) * 6 * chans**3, transcendentals=0, bytes_accessed=len(chunks) * 6 * chans**2
            ),
            name="rest",
        )(*far_memory(z), out_weight)

    up_sum, down_sum = turn(out_up, 1), turn(out_down, -1)
    nothing = jnp.zeros_like(up_sum, f32)
    up_sum = jnp.stack([up_sum.astype(f32), nothing])
    down_sum = jnp.stack([nothing, down_sum.astype(f32)])
    parts = rest(z, (3, -3))
    for hop in (2, 1, 0):
        ups_now = (parts[0].astype(f32) + up_sum).astype(bf16)
        downs_now = (parts[1].astype(f32) + down_sum).astype(bf16)
        _, _, z = lax.optimization_barrier((ups_now, downs_now, z))
        up_sum, down_sum = turn(ups_now, 1).astype(f32), turn(downs_now, -1).astype(f32)
        parts = rest(z, (hop, -hop) if hop else (0,))
    total = parts[0].astype(f32) + up_sum + down_sum
    other = across(total[1].astype(bf16))
    return (total[0] + other.astype(f32)).astype(bf16)


def solution(mesh):
    in_specs = (
        P("seq", "tp"),
        P(),
        P(None, "tp"),
        P(None, "tp"),
        P(None, "tp"),
        P(None, "tp"),
        P(None, "tp"),
        P(None, "tp"),
        P("tp", None),
    )
    out_specs = P("seq", "tp")
    return jax.shard_map(body, mesh=mesh, in_specs=in_specs, out_specs=out_specs, check_vma=False)
```

```python
import functools
import jax
import jax.numpy as jnp
from jax import lax
from jax.experimental import pallas as pl
from jax.experimental.pallas import tpu as pltpu
from jax.sharding import PartitionSpec as P

eps = 1e-05
f32 = jnp.float32
bf16 = jnp.bfloat16
T = 16


def tables_kernel(rates_ref, residues_ref, pow_ref, near_ref, fore_ref, back_ref):
    rates = rates_ref[...]
    modes, chans = rates.shape
    strength = residues_ref[...] * jnp.sqrt(rates)
    for k in range(T):
        pow_ref[k] = jnp.exp(-rates * float(k))
    pow_ref[T] = jnp.exp(-rates * float(T))
    pow_ref[T + 1] = jnp.exp(rates)
    steps = lax.broadcasted_iota(jnp.int32, (T, chans), 0).astype(f32)
    total = jnp.zeros((T, chans), f32)
    for m in range(modes):
        rate = rates[m : m + 1, :]
        weight = strength[m : m + 1, :]
        fore = weight * jnp.exp(-rate * (steps + 1.0))
        fore_ref[m] = fore
        back_ref[m] = weight * jnp.exp(-rate * (float(T) - steps))
        total = total + fore
    near_ref[pl.ds(T + 1, T), :] = total
    near_ref[pl.ds(T, 1), :] = jnp.sum(strength, axis=0, keepdims=True)
    for k in range(1, T + 1):
        near_ref[pl.ds(T - k, 1), :] = total[k - 1 : k, :]


def reversal(n):
    i0 = lax.broadcasted_iota(jnp.int32, (n, n), 0)
    i1 = lax.broadcasted_iota(jnp.int32, (n, n), 1)
    return (i0 + i1 == n - 1).astype(f32).astype(bf16)


def shard_at(place, column, hop, tp):
    ring = tp // 2
    return ((place // ring + column) % 2) * ring + (place % ring + hop + ring) % ring


def rows_of(block, size):
    return pl.ds(pl.multiple_of(block * size, size), size)


def accumulate(slots, x_refs, gain_ref, weights, x_buf, w_buf, sems, acc_ref, sq_ref, carried=(), sinks=()):
    tp = lax.axis_size("tp")
    place = lax.axis_index("tp")
    rows, chans = x_buf.shape[1:]
    last = len(slots)
    copies = []
    for n, (array, entry, column, hop) in enumerate(slots):
        block = shard_at(place, column, hop, tp)
        source = x_refs[array] if entry is None else x_refs[array].at[entry]
        group = [pltpu.make_async_copy(source, x_buf.at[n], sems.at[n, 0])]
        for w, ref in enumerate(weights):
            lanes = pl.ds(w * chans, chans)
            group.append(
                pltpu.make_async_copy(ref.at[rows_of(block, chans), :], w_buf.at[n, 0, :, lanes], sems.at[n, 1 + w])
            )
            group.append(
                pltpu.make_async_copy(
                    ref.at[rows_of(tp - 1 - block, chans), :], w_buf.at[n, 1, :, lanes], sems.at[n, 3 + w]
                )
            )
        for copy in group:
            copy.start()
        copies.append(group)
        if n == 0 and carried:
            acc_in, sq_in = carried
            before = [
                pltpu.make_async_copy(acc_in.at[0], acc_ref.at[0], sems.at[last, 0]),
                pltpu.make_async_copy(acc_in.at[1], acc_ref.at[1], sems.at[last, 1]),
                pltpu.make_async_copy(sq_in, sq_ref, sems.at[last, 2]),
            ]
            for copy in before:
                copy.start()
    flip = reversal(chans)
    after = []

    def leave(index, source, sink, ready):
        if sinks and ready:
            copy = pltpu.make_async_copy(source, sink, sems.at[last + 1, index])
            copy.start()
            after.append(copy)

    for n, (array, entry, column, hop) in enumerate(slots):
        block = shard_at(place, column, hop, tp)
        for copy in copies[n]:
            copy.wait()
        x = x_buf[n]
        part = x.astype(f32)
        square = part * part
        square = sum(square[:, i : i + 128] for i in range(0, chans, 128))
        mirrored = jnp.dot(x, flip, preferred_element_type=f32)
        own = (part * gain_ref[block]).astype(bf16)
        far = (mirrored * gain_ref[tp - 1 - block]).astype(bf16)
        first = jnp.dot(own, w_buf[n, 0], preferred_element_type=f32)
        if n == 0 and carried:
            for copy in before:
                copy.wait()
        fresh = n == 0 and not carried
        done = n == last - 1
        acc_ref[0] = first if fresh else acc_ref[0] + first
        sq_ref[...] = square if fresh else sq_ref[...] + square
        if sinks:
            leave(0, acc_ref.at[0], sinks[0].at[0], done)
            leave(2, sq_ref, sinks[1], done)
        second = jnp.dot(far, w_buf[n, 1], preferred_element_type=f32)
        acc_ref[1] = second if fresh else acc_ref[1] + second
        if sinks:
            leave(1, acc_ref.at[1], sinks[0].at[1], done)
    for copy in after:
        copy.wait()


def early_kernel(slots, arrays, more, *refs):
    x_refs, refs = refs[:arrays], refs[arrays:]
    gain_ref, wv_ref, wg_ref, refs = refs[0], refs[1], refs[2], refs[3:]
    carried, sinks, refs = refs[:more], refs[more : more + 2], refs[more + 2 :]
    acc_ref, sq_ref, x_buf, w_buf, sems = refs
    accumulate(slots, x_refs, gain_ref, (wv_ref, wg_ref), x_buf, w_buf, sems, acc_ref, sq_ref, carried, sinks)


def states_kernel(slots, arrays, *refs):
    x_refs, refs = refs[:arrays], refs[arrays:]
    gain_ref, wv_ref, wg_ref, acc_in, sq_in, vt_ref, pow_ref, refs = *refs[:7], refs[7:]
    send_ref, sv_ref, gates_ref, edge_ref, refs = *refs[:4], refs[4:]
    acc_ref, sq_ref, pad_ref, x_buf, w_buf, sems = refs
    accumulate(
        slots, x_refs, gain_ref, (wv_ref, wg_ref), x_buf, w_buf, sems, acc_ref, sq_ref, (acc_in, sq_in)
    )
    rows, chans = x_buf.shape[1:]
    place = lax.axis_index("seq")
    places = lax.axis_size("seq")
    mean = jnp.sum(sq_ref[...], axis=1, keepdims=True) * (1.0 / (lax.axis_size("tp") * chans))
    scale = lax.rsqrt(mean + eps)
    low_ok = (place > 0).astype(f32)
    high_ok = (place < places - 1).astype(f32)
    zeros8 = jnp.zeros((8, chans), f32)
    tiles = rows // T
    for s in range(2):
        strand = slice(s * chans, (s + 1) * chans)
        gates = acc_ref[s, :, chans:] * scale
        gates_ref[:, strand] = gates
        for g in range(chans // 128):
            row = s * (chans // 128) + g
            first = gates[0:1, g * 128 : (g + 1) * 128]
            last = gates[rows - 1 : rows, g * 128 : (g + 1) * 128]
            for i in range(places):
                send_ref[i, row : row + 1, 2 * chans :] = jnp.where(i > place, last, first)
        v = acc_ref[s, :, :chans] * scale
        pad_ref[0:8, :] = zeros8
        pad_ref[8 : 8 + rows, :] = v
        pad_ref[8 + rows : 16 + rows, :] = zeros8
        a, c = (0, 2) if s == 0 else (2, 0)
        ta, tb, tc = vt_ref[a : a + 1, :], vt_ref[1:2, :], vt_ref[c : c + 1, :]
        sv = ta * pad_ref[7 : 7 + rows, :] + tb * v + tc * pad_ref[9 : 9 + rows, :]
        sv_ref[s] = sv.reshape(tiles, T, chans)
        all_low = tc * v[0:1, :] * low_ok
        all_high = ta * v[rows - 1 : rows, :] * high_ok
        edge_ref[s, 0] = jnp.broadcast_to(all_low, (8, chans))
        edge_ref[s, 1] = jnp.broadcast_to(all_high, (8, chans))
        for g in range(chans // 128):
            lanes = slice(g * 128, (g + 1) * 128)
            low, high = all_low[:, lanes], all_high[:, lanes]
            jump = pow_ref[T, :, lanes]
            inverse = pow_ref[T + 1, :, lanes]
            fold = jnp.zeros((tiles, 16, 128), f32)
            for j in range(T):
                fold = fold + pow_ref[T - 1 - j, :, lanes][None] * sv_ref[s, :, j : j + 1, lanes]
            state = jnp.broadcast_to(low, (16, 128))
            for n in range(tiles):
                state = jump * state + fold[n]
            ahead = state + inverse * high
            fold = jnp.zeros((tiles, 16, 128), f32)
            for j in range(T):
                fold = fold + pow_ref[j, :, lanes][None] * sv_ref[s, :, j : j + 1, lanes]
            state = jnp.broadcast_to(high, (16, 128))
            for n in reversed(range(tiles)):
                state = jump * state + fold[n]
            behind = state + inverse * low
            wide = slice(s * chans + g * 128, s * chans + (g + 1) * 128)
            for i in range(places):
                send_ref[i, :, wide] = jnp.where(i > place, ahead, behind)


def spread(conv, spread_f_ref, spread_b_ref, st_ref, lanes):
    for m in range(16):
        conv = conv + spread_f_ref[m, :, lanes][None] * st_ref[0, :, m : m + 1, :]
    for m in range(16):
        conv = conv + spread_b_ref[m, :, lanes][None] * st_ref[1, :, m : m + 1, :]
    return conv


def local_kernel(sv_ref, edge_ref, pow_ref, near_ref, spread_f_ref, spread_b_ref, local_ref, st_ref):
    tiles = sv_ref.shape[1]
    chans = sv_ref.shape[3]
    for s in range(2):
        for g in range(chans // 128):
            lanes = slice(g * 128, (g + 1) * 128)
            jump = pow_ref[T, :, lanes]
            fold = jnp.zeros((tiles, 16, 128), f32)
            for j in range(T):
                fold = fold + pow_ref[T - 1 - j, :, lanes][None] * sv_ref[s, :, j : j + 1, lanes]
            state = jnp.broadcast_to(edge_ref[s, 0, 0:1, lanes], (16, 128))
            for n in range(tiles):
                st_ref[0, n] = state
                state = jump * state + fold[n]
            fold = jnp.zeros((tiles, 16, 128), f32)
            for j in range(T):
                fold = fold + pow_ref[j, :, lanes][None] * sv_ref[s, :, j : j + 1, lanes]
            state = jnp.broadcast_to(edge_ref[s, 1, 0:1, lanes], (16, 128))
            for n in reversed(range(tiles)):
                st_ref[1, n] = state
                state = jump * state + fold[n]
            conv = jnp.zeros((tiles, T, 128), f32)
            for j in range(T):
                conv = conv + near_ref[T - j : 2 * T - j, lanes][None] * sv_ref[s, :, j : j + 1, lanes]
            local_ref[s, :, :, lanes] = spread(conv, spread_f_ref, spread_b_ref, st_ref, lanes)


def fetch_columns(chunks, wo_ref, w_buf, sems):
    tp = lax.axis_size("tp")
    place = lax.axis_index("tp")
    chans = w_buf.shape[2]
    copies = []
    for n, (column, hop) in enumerate(chunks):
        block = shard_at(place, column, hop, tp)
        pair = (
            pltpu.make_async_copy(wo_ref.at[:, rows_of(block, chans)], w_buf.at[n, 0], sems.at[n, 0]),
            pltpu.make_async_copy(wo_ref.at[:, rows_of(tp - 1 - block, chans)], w_buf.at[n, 1], sems.at[n, 1]),
        )
        for copy in pair:
            copy.start()
        copies.append(pair)
    return copies


def partial_chunk(n, copies, z_ref, w_buf, flip):
    chans = w_buf.shape[2]
    for copy in copies[n]:
        copy.wait()
    far = jnp.dot(w_buf[n, 1], flip, preferred_element_type=f32).astype(bf16)
    out = jnp.dot(z_ref[:, :chans], w_buf[n, 0], preferred_element_type=f32)
    return out + jnp.dot(z_ref[:, chans:], far, preferred_element_type=f32)


def gated_kernel(
    chunks, recv_ref, local_ref, gates_ref, gt_ref, rates_ref,
    spread_f_ref, spread_b_ref, wo_ref, z_ref, *refs,
):
    outs, (pad_ref, st_ref, w_buf, sems) = refs[: len(chunks)], refs[len(chunks) :]
    rows = gates_ref.shape[0]
    chans = gates_ref.shape[1] // 2
    tiles = rows // T
    place = lax.axis_index("seq")
    places = lax.axis_size("seq")
    low_ok = (place > 0).astype(f32)
    high_ok = (place < places - 1).astype(f32)
    below = jnp.maximum(place - 1, 0)
    above = jnp.minimum(place + 1, places - 1)
    copies = fetch_columns(chunks, wo_ref, w_buf, sems)
    for s in range(2):
        wide = slice(s * chans, (s + 1) * chans)
        g = gates_ref[:, wide]
        pad_ref[8 : 8 + rows, :] = g
        for g2 in range(chans // 128):
            row = s * (chans // 128) + g2
            lanes = slice(g2 * 128, (g2 + 1) * 128)
            pad_ref[7:8, lanes] = recv_ref[below, row : row + 1, 2 * chans :] * low_ok
            pad_ref[8 + rows : 9 + rows, lanes] = recv_ref[above, row : row + 1, 2 * chans :] * high_ok
        a, c = (0, 2) if s == 0 else (2, 0)
        ta, tb, tc = gt_ref[a : a + 1, :], gt_ref[1:2, :], gt_ref[c : c + 1, :]
        sg = ta * pad_ref[7 : 7 + rows, :] + tb * g + tc * pad_ref[9 : 9 + rows, :]
        for g2 in range(chans // 128):
            lanes = slice(g2 * 128, (g2 + 1) * 128)
            wide = slice(s * chans + g2 * 128, s * chans + (g2 + 1) * 128)
            rates = rates_ref[:, lanes]
            hop = jnp.exp(-rates * float(rows))
            jump = jnp.exp(-rates * float(T))
            carry_f = jnp.zeros((16, 128), f32)
            carry_b = jnp.zeros((16, 128), f32)
            for j in range(places):
                r = places - 1 - j
                carry_f = jnp.where(j < place, carry_f * hop + recv_ref[j, :, wide], carry_f)
                carry_b = jnp.where(r > place, carry_b * hop + recv_ref[r, :, wide], carry_b)
            for n in range(tiles):
                m = tiles - 1 - n
                st_ref[0, n] = carry_f
                st_ref[1, m] = carry_b
                carry_f = carry_f * jump
                carry_b = carry_b * jump
            conv = spread(local_ref[s, :, :, lanes], spread_f_ref, spread_b_ref, st_ref, lanes)
            z_ref[:, wide] = (sg[:, lanes] * conv.reshape(rows, 128)).astype(bf16)
    flip = reversal(chans)
    for n, ref in enumerate(outs):
        ref[...] = partial_chunk(n, copies, z_ref, w_buf, flip).astype(bf16)


def rest_kernel(chunks, z_ref, wo_ref, *refs):
    outs, (z_buf, w_buf, sems) = refs[:-3], refs[-3:]
    arrive = pltpu.make_async_copy(z_ref, z_buf, sems.at[len(chunks), 0])
    arrive.start()
    copies = fetch_columns(chunks, wo_ref, w_buf, sems)
    flip = reversal(w_buf.shape[2])
    arrive.wait()
    for n in range(len(chunks)):
        outs[n // 2][n % 2] = partial_chunk(n, copies, z_buf, w_buf, flip).astype(bf16)


def far_memory(*arrays):
    return [pltpu.with_memory_space_constraint(a, pltpu.HBM) for a in arrays]


def whole(shape):
    return pl.BlockSpec(shape, lambda *_: (0,) * len(shape))


remote = pl.BlockSpec(memory_space=pl.ANY)


def body(
    hidden, norm_gain, value_weight, gate_weight, value_taps, gate_taps, rates, residues, out_weight
):
    rows, chans = hidden.shape
    tp = lax.axis_size("tp")
    ring = tp // 2
    places = lax.axis_size("seq")
    modes = rates.shape[0]
    tiles = rows // T
    shape = pltpu.HBM
    params = pltpu.CompilerParams(vmem_limit_bytes=24 << 20)

    def turn(a, hop):
        return lax.ppermute(
            a, "tp", [(c * ring + i, c * ring + (i + hop) % ring) for c in range(2) for i in range(ring)]
        )

    def across(a):
        return lax.ppermute(a, "tp", [(i, (i + ring) % tp) for i in range(tp)])

    rates, residues = far_memory(rates, residues)
    powers, near, spread_f, spread_b = pl.pallas_call(
        tables_kernel,
        out_shape=(
            shape((T + 2, modes, chans), f32),
            shape((2 * T + 8, chans), f32),
            shape((modes, T, chans), f32),
            shape((modes, T, chans), f32),
        ),
        compiler_params=params,
        name="tables",
    )(rates, residues)
    gain = norm_gain.reshape(tp, 1, chans)
    value_weight, gate_weight, out_weight = far_memory(value_weight, gate_weight, out_weight)
    gain, value_taps, gate_taps = far_memory(gain, value_taps, gate_taps)

    def project(arrays, slots, carried):
        return pl.pallas_call(
            functools.partial(early_kernel, slots, len(arrays), len(carried)),
            in_specs=[remote] * len(arrays) + [whole(gain.shape), remote, remote] + [remote] * len(carried),
            out_specs=[remote, remote],
            out_shape=(shape((2, rows, 2 * chans), f32), shape((rows, 128), f32)),
            scratch_shapes=[
                pltpu.VMEM((2, rows, 2 * chans), f32),
                pltpu.VMEM((rows, 128), f32),
                pltpu.VMEM((len(slots), rows, chans), bf16),
                pltpu.VMEM((len(slots), 2, chans, 2 * chans), bf16),
                pltpu.SemaphoreType.DMA((len(slots) + 2, 5)),
            ],
            compiler_params=params,
            cost_estimate=pl.CostEstimate(
                flops=len(slots) * 10 * chans**3, transcendentals=0, bytes_accessed=len(slots) * 10 * chans**2
            ),
            name="project",
        )(*arrays, gain, value_weight, gate_weight, *carried)

    def pair_slots(hops):
        return tuple((n, c, c, hop) for n, hop in enumerate(hops) for c in range(2))

    start = jnp.stack([hidden, across(hidden)])
    up1, down1 = turn(start, 1), turn(start, -1)
    up1, powers, near, spread_f, spread_b = lax.optimization_barrier((up1, powers, near, spread_f, spread_b))
    up2, down2 = turn(up1, 1), turn(down1, -1)
    carried = project([start, up1, down1], pair_slots((0, -1, 1)), ())
    up2, carried = lax.optimization_barrier((up2, carried))
    up3, down3 = turn(up2, 1), turn(down2, -1)
    carried = project([up2, down2], pair_slots((-2, 2)), far_memory(*carried))
    up3, carried = lax.optimization_barrier((up3, carried))
    last_up, last_down = turn(up3[0], 1), turn(down3[1], -1)
    carried = project([up3, down3], pair_slots((-3, 3)), far_memory(*carried))

    slots = ((0, None, 0, -4), (1, None, 1, 4))
    send, sv, gates, edge = pl.pallas_call(
        functools.partial(states_kernel, slots, 2),
        in_specs=[remote, remote, whole(gain.shape), remote, remote, remote, remote]
        + [whole(value_taps.shape), whole(powers.shape)],
        out_specs=[
            whole((places, modes, 2 * chans + 128)),
            whole((2, tiles, T, chans)),
            whole((rows, 2 * chans)),
            whole((2, 2, 8, chans)),
        ],
        out_shape=(
            shape((places, modes, 2 * chans + 128), f32),
            shape((2, tiles, T, chans), f32),
            shape((rows, 2 * chans), f32),
            shape((2, 2, 8, chans), f32),
        ),
        scratch_shapes=[
            pltpu.VMEM((2, rows, 2 * chans), f32),
            pltpu.VMEM((rows, 128), f32),
            pltpu.VMEM((rows + 16, chans), f32),
            pltpu.VMEM((2, rows, chans), bf16),
            pltpu.VMEM((2, 2, chans, 2 * chans), bf16),
            pltpu.SemaphoreType.DMA((4, 5)),
        ],
        compiler_params=params,
        name="states",
    )(
        last_up, last_down, gain, value_weight, gate_weight, *far_memory(*carried), value_taps,
        *far_memory(powers),
    )

    recv = lax.all_to_all(send, "seq", split_axis=0, concat_axis=0)
    local = pl.pallas_call(
        local_kernel,
        out_shape=shape((2, tiles, T, chans), f32),
        scratch_shapes=[pltpu.VMEM((2, tiles, modes, 128), f32)],
        compiler_params=params,
        name="local",
    )(*far_memory(sv, edge, powers, near, spread_f, spread_b))

    chunks = ((0, 4), (1, 4))
    square = shape((rows, chans), bf16)
    pair = shape((2, rows, chans), bf16)
    inputs = (
        recv, *far_memory(local, gates), gate_taps, rates,
        *far_memory(spread_f, spread_b),
    )
    z, out_up, out_down = pl.pallas_call(
        functools.partial(gated_kernel, chunks),
        in_specs=[whole(a.shape) for a in inputs] + [remote],
        out_specs=[whole((rows, 2 * chans)), whole((rows, chans)), whole((rows, chans))],
        out_shape=(shape((rows, 2 * chans), bf16), square, square),
        scratch_shapes=[
            pltpu.VMEM((rows + 16, chans), f32),
            pltpu.VMEM((2, tiles, modes, 128), f32),
            pltpu.VMEM((len(chunks), 2, chans, chans), bf16),
            pltpu.SemaphoreType.DMA((len(chunks), 2)),
        ],
        compiler_params=params,
        name="gated",
    )(*inputs, out_weight)

    def rest(z, hops):
        chunks = tuple((c, hop) for hop in hops for c in range(2))
        return pl.pallas_call(
            functools.partial(rest_kernel, chunks),
            in_specs=[remote, remote],
            out_specs=[whole((2, rows, chans))] * len(hops),
            out_shape=(pair,) * len(hops),
            scratch_shapes=[
                pltpu.VMEM(z.shape, bf16),
                pltpu.VMEM((len(chunks), 2, chans, chans), bf16),
                pltpu.SemaphoreType.DMA((len(chunks) + 1, 2)),
            ],
            compiler_params=params,
            cost_estimate=pl.CostEstimate(
                flops=len(chunks) * 6 * chans**3, transcendentals=0, bytes_accessed=len(chunks) * 6 * chans**2
            ),
            name="rest",
        )(*far_memory(z), out_weight)

    up_sum, down_sum = turn(out_up, 1), turn(out_down, -1)
    nothing = jnp.zeros_like(up_sum, f32)
    up_sum = jnp.stack([up_sum.astype(f32), nothing])
    down_sum = jnp.stack([nothing, down_sum.astype(f32)])
    parts = rest(z, (3, -3))
    for hop in (2, 1, 0):
        ups_now = (parts[0].astype(f32) + up_sum).astype(bf16)
        downs_now = (parts[1].astype(f32) + down_sum).astype(bf16)
        _, _, z = lax.optimization_barrier((ups_now, downs_now, z))
        up_sum, down_sum = turn(ups_now, 1).astype(f32), turn(downs_now, -1).astype(f32)
        parts = rest(z, (hop, -hop) if hop else (0,))
    total = parts[0].astype(f32) + up_sum + down_sum
    other = across(total[1].astype(bf16))
    return (total[0] + other.astype(f32)).astype(bf16)


def solution(mesh):
    in_specs = (
        P("seq", "tp"),
        P(),
        P(None, "tp"),
        P(None, "tp"),
        P(None, "tp"),
        P(None, "tp"),
        P(None, "tp"),
        P(None, "tp"),
        P("tp", None),
    )
    out_specs = P("seq", "tp")
    return jax.shard_map(body, mesh=mesh, in_specs=in_specs, out_specs=out_specs, check_vma=False)
```

```python
import functools
import jax
import jax.numpy as jnp
from jax import lax
from jax.experimental import pallas as pl
from jax.experimental.pallas import tpu as pltpu
from jax.sharding import PartitionSpec as P

eps = 1e-05
f32 = jnp.float32
bf16 = jnp.bfloat16
T = 16


def tables_kernel(rates_ref, residues_ref, pow_ref, near_ref, fore_ref, back_ref):
    rates = rates_ref[...]
    modes, chans = rates.shape
    strength = residues_ref[...] * jnp.sqrt(rates)
    for k in range(T):
        pow_ref[k] = jnp.exp(-rates * float(k))
    pow_ref[T] = jnp.exp(-rates * float(T))
    pow_ref[T + 1] = jnp.exp(rates)
    steps = lax.broadcasted_iota(jnp.int32, (T, chans), 0).astype(f32)
    total = jnp.zeros((T, chans), f32)
    for m in range(modes):
        rate = rates[m : m + 1, :]
        weight = strength[m : m + 1, :]
        fore = weight * jnp.exp(-rate * (steps + 1.0))
        fore_ref[m] = fore
        back_ref[m] = weight * jnp.exp(-rate * (float(T) - steps))
        total = total + fore
    near_ref[pl.ds(T + 1, T), :] = total
    near_ref[pl.ds(T, 1), :] = jnp.sum(strength, axis=0, keepdims=True)
    for k in range(1, T + 1):
        near_ref[pl.ds(T - k, 1), :] = total[k - 1 : k, :]


def reversal(n):
    i0 = lax.broadcasted_iota(jnp.int32, (n, n), 0)
    i1 = lax.broadcasted_iota(jnp.int32, (n, n), 1)
    return (i0 + i1 == n - 1).astype(f32).astype(bf16)


def shard_at(place, column, hop, tp):
    ring = tp // 2
    return ((place // ring + column) % 2) * ring + (place % ring + hop + ring) % ring


def rows_of(block, size):
    return pl.ds(pl.multiple_of(block * size, size), size)


def accumulate(slots, x_refs, gain_ref, weights, x_buf, w_buf, sems, acc_ref, sq_ref, carried=(), sinks=()):
    tp = lax.axis_size("tp")
    place = lax.axis_index("tp")
    rows, chans = x_buf.shape[1:]
    last = len(slots)
    copies = []
    for n, (array, entry, column, hop) in enumerate(slots):
        block = shard_at(place, column, hop, tp)
        source = x_refs[array] if entry is None else x_refs[array].at[entry]
        group = [pltpu.make_async_copy(source, x_buf.at[n], sems.at[n, 0])]
        for w, ref in enumerate(weights):
            lanes = pl.ds(w * chans, chans)
            group.append(
                pltpu.make_async_copy(ref.at[rows_of(block, chans), :], w_buf.at[n, 0, :, lanes], sems.at[n, 1 + w])
            )
            group.append(
                pltpu.make_async_copy(
                    ref.at[rows_of(tp - 1 - block, chans), :], w_buf.at[n, 1, :, lanes], sems.at[n, 3 + w]
                )
            )
        for copy in group:
            copy.start()
        copies.append(group)
        if n == 0 and carried:
            acc_in, sq_in = carried
            before = [
                pltpu.make_async_copy(acc_in.at[0], acc_ref.at[0], sems.at[last, 0]),
                pltpu.make_async_copy(acc_in.at[1], acc_ref.at[1], sems.at[last, 1]),
                pltpu.make_async_copy(sq_in, sq_ref, sems.at[last, 2]),
            ]
            for copy in before:
                copy.start()
    flip = reversal(chans)
    after = []

    def leave(index, source, sink, ready):
        if sinks and ready:
            copy = pltpu.make_async_copy(source, sink, sems.at[last + 1, index])
            copy.start()
            after.append(copy)

    for n, (array, entry, column, hop) in enumerate(slots):
        block = shard_at(place, column, hop, tp)
        for copy in copies[n]:
            copy.wait()
        x = x_buf[n]
        part = x.astype(f32)
        square = part * part
        square = sum(square[:, i : i + 128] for i in range(0, chans, 128))
        mirrored = jnp.dot(x, flip, preferred_element_type=f32)
        own = (part * gain_ref[block]).astype(bf16)
        far = (mirrored * gain_ref[tp - 1 - block]).astype(bf16)
        first = jnp.dot(own, w_buf[n, 0], preferred_element_type=f32)
        if n == 0 and carried:
            for copy in before:
                copy.wait()
        fresh = n == 0 and not carried
        done = n == last - 1
        acc_ref[0] = first if fresh else acc_ref[0] + first
        sq_ref[...] = square if fresh else sq_ref[...] + square
        if sinks:
            leave(0, acc_ref.at[0], sinks[0].at[0], done)
            leave(2, sq_ref, sinks[1], done)
        second = jnp.dot(far, w_buf[n, 1], preferred_element_type=f32)
        acc_ref[1] = second if fresh else acc_ref[1] + second
        if sinks:
            leave(1, acc_ref.at[1], sinks[0].at[1], done)
    for copy in after:
        copy.wait()


def early_kernel(slots, arrays, more, *refs):
    x_refs, refs = refs[:arrays], refs[arrays:]
    gain_ref, wv_ref, wg_ref, refs = refs[0], refs[1], refs[2], refs[3:]
    carried, sinks, refs = refs[:more], refs[more : more + 2], refs[more + 2 :]
    acc_ref, sq_ref, x_buf, w_buf, sems = refs
    accumulate(slots, x_refs, gain_ref, (wv_ref, wg_ref), x_buf, w_buf, sems, acc_ref, sq_ref, carried, sinks)


def states_kernel(slots, arrays, *refs):
    x_refs, refs = refs[:arrays], refs[arrays:]
    gain_ref, wv_ref, wg_ref, acc_in, sq_in, vt_ref, pow_ref, refs = *refs[:7], refs[7:]
    send_ref, sv_ref, gates_ref, edge_ref, refs = *refs[:4], refs[4:]
    acc_ref, sq_ref, pad_ref, x_buf, w_buf, sems = refs
    accumulate(
        slots, x_refs, gain_ref, (wv_ref, wg_ref), x_buf, w_buf, sems, acc_ref, sq_ref, (acc_in, sq_in)
    )
    rows, chans = x_buf.shape[1:]
    place = lax.axis_index("seq")
    places = lax.axis_size("seq")
    mean = jnp.sum(sq_ref[...], axis=1, keepdims=True) * (1.0 / (lax.axis_size("tp") * chans))
    scale = lax.rsqrt(mean + eps)
    low_ok = (place > 0).astype(f32)
    high_ok = (place < places - 1).astype(f32)
    zeros8 = jnp.zeros((8, chans), f32)
    tiles = rows // T
    for s in range(2):
        strand = slice(s * chans, (s + 1) * chans)
        gates = acc_ref[s, :, chans:] * scale
        gates_ref[:, strand] = gates
        for g in range(chans // 128):
            row = s * (chans // 128) + g
            first = gates[0:1, g * 128 : (g + 1) * 128]
            last = gates[rows - 1 : rows, g * 128 : (g + 1) * 128]
            for i in range(places):
                send_ref[i, row : row + 1, 2 * chans :] = jnp.where(i > place, last, first)
        v = acc_ref[s, :, :chans] * scale
        pad_ref[0:8, :] = zeros8
        pad_ref[8 : 8 + rows, :] = v
        pad_ref[8 + rows : 16 + rows, :] = zeros8
        a, c = (0, 2) if s == 0 else (2, 0)
        ta, tb, tc = vt_ref[a : a + 1, :], vt_ref[1:2, :], vt_ref[c : c + 1, :]
        sv = ta * pad_ref[7 : 7 + rows, :] + tb * v + tc * pad_ref[9 : 9 + rows, :]
        sv_ref[s] = sv.reshape(tiles, T, chans)
        all_low = tc * v[0:1, :] * low_ok
        all_high = ta * v[rows - 1 : rows, :] * high_ok
        edge_ref[s, 0] = jnp.broadcast_to(all_low, (8, chans))
        edge_ref[s, 1] = jnp.broadcast_to(all_high, (8, chans))
        for g in range(chans // 128):
            lanes = slice(g * 128, (g + 1) * 128)
            low, high = all_low[:, lanes], all_high[:, lanes]
            jump = pow_ref[T, :, lanes]
            inverse = pow_ref[T + 1, :, lanes]
            fold = jnp.zeros((tiles, 16, 128), f32)
            for j in range(T):
                fold = fold + pow_ref[T - 1 - j, :, lanes][None] * sv_ref[s, :, j : j + 1, lanes]
            state = jnp.broadcast_to(low, (16, 128))
            for n in range(tiles):
                state = jump * state + fold[n]
            ahead = state + inverse * high
            fold = jnp.zeros((tiles, 16, 128), f32)
            for j in range(T):
                fold = fold + pow_ref[j, :, lanes][None] * sv_ref[s, :, j : j + 1, lanes]
            state = jnp.broadcast_to(high, (16, 128))
            for n in reversed(range(tiles)):
                state = jump * state + fold[n]
            behind = state + inverse * low
            wide = slice(s * chans + g * 128, s * chans + (g + 1) * 128)
            for i in range(places):
                send_ref[i, :, wide] = jnp.where(i > place, ahead, behind)


def spread(conv, spread_f_ref, spread_b_ref, st_ref, lanes):
    for m in range(16):
        conv = conv + spread_f_ref[m, :, lanes][None] * st_ref[0, :, m : m + 1, :]
    for m in range(16):
        conv = conv + spread_b_ref[m, :, lanes][None] * st_ref[1, :, m : m + 1, :]
    return conv


def local_kernel(sv_ref, edge_ref, pow_ref, near_ref, spread_f_ref, spread_b_ref, local_ref, st_ref):
    tiles = sv_ref.shape[1]
    chans = sv_ref.shape[3]
    for s in range(2):
        for g in range(chans // 128):
            lanes = slice(g * 128, (g + 1) * 128)
            jump = pow_ref[T, :, lanes]
            fold = jnp.zeros((tiles, 16, 128), f32)
            for j in range(T):
                fold = fold + pow_ref[T - 1 - j, :, lanes][None] * sv_ref[s, :, j : j + 1, lanes]
            state = jnp.broadcast_to(edge_ref[s, 0, 0:1, lanes], (16, 128))
            for n in range(tiles):
                st_ref[0, n] = state
                state = jump * state + fold[n]
            fold = jnp.zeros((tiles, 16, 128), f32)
            for j in range(T):
                fold = fold + pow_ref[j, :, lanes][None] * sv_ref[s, :, j : j + 1, lanes]
            state = jnp.broadcast_to(edge_ref[s, 1, 0:1, lanes], (16, 128))
            for n in reversed(range(tiles)):
                st_ref[1, n] = state
                state = jump * state + fold[n]
            conv = jnp.zeros((tiles, T, 128), f32)
            for j in range(T):
                conv = conv + near_ref[T - j : 2 * T - j, lanes][None] * sv_ref[s, :, j : j + 1, lanes]
            local_ref[s, :, :, lanes] = spread(conv, spread_f_ref, spread_b_ref, st_ref, lanes)


def fetch_columns(chunks, wo_ref, w_buf, sems):
    tp = lax.axis_size("tp")
    place = lax.axis_index("tp")
    chans = w_buf.shape[2]
    copies = []
    for n, (column, hop) in enumerate(chunks):
        block = shard_at(place, column, hop, tp)
        pair = (
            pltpu.make_async_copy(wo_ref.at[:, rows_of(block, chans)], w_buf.at[n, 0], sems.at[n, 0]),
            pltpu.make_async_copy(wo_ref.at[:, rows_of(tp - 1 - block, chans)], w_buf.at[n, 1], sems.at[n, 1]),
        )
        for copy in pair:
            copy.start()
        copies.append(pair)
    return copies


def partial_chunk(n, copies, z_ref, w_buf, flip):
    chans = w_buf.shape[2]
    for copy in copies[n]:
        copy.wait()
    far = jnp.dot(w_buf[n, 1], flip, preferred_element_type=f32).astype(bf16)
    out = jnp.dot(z_ref[:, :chans], w_buf[n, 0], preferred_element_type=f32)
    return out + jnp.dot(z_ref[:, chans:], far, preferred_element_type=f32)


def gated_kernel(
    chunks, recv_ref, local_ref, gates_ref, gt_ref, rates_ref,
    spread_f_ref, spread_b_ref, wo_ref, z_ref, *refs,
):
    outs, (pad_ref, st_ref, w_buf, sems) = refs[: len(chunks)], refs[len(chunks) :]
    rows = gates_ref.shape[0]
    chans = gates_ref.shape[1] // 2
    tiles = rows // T
    place = lax.axis_index("seq")
    places = lax.axis_size("seq")
    low_ok = (place > 0).astype(f32)
    high_ok = (place < places - 1).astype(f32)
    below = jnp.maximum(place - 1, 0)
    above = jnp.minimum(place + 1, places - 1)
    copies = fetch_columns(chunks, wo_ref, w_buf, sems)
    for s in range(2):
        wide = slice(s * chans, (s + 1) * chans)
        g = gates_ref[:, wide]
        pad_ref[8 : 8 + rows, :] = g
        for g2 in range(chans // 128):
            row = s * (chans // 128) + g2
            lanes = slice(g2 * 128, (g2 + 1) * 128)
            pad_ref[7:8, lanes] = recv_ref[below, row : row + 1, 2 * chans :] * low_ok
            pad_ref[8 + rows : 9 + rows, lanes] = recv_ref[above, row : row + 1, 2 * chans :] * high_ok
        a, c = (0, 2) if s == 0 else (2, 0)
        ta, tb, tc = gt_ref[a : a + 1, :], gt_ref[1:2, :], gt_ref[c : c + 1, :]
        sg = ta * pad_ref[7 : 7 + rows, :] + tb * g + tc * pad_ref[9 : 9 + rows, :]
        for g2 in range(chans // 128):
            lanes = slice(g2 * 128, (g2 + 1) * 128)
            wide = slice(s * chans + g2 * 128, s * chans + (g2 + 1) * 128)
            rates = rates_ref[:, lanes]
            hop = jnp.exp(-rates * float(rows))
            jump = jnp.exp(-rates * float(T))
            carry_f = jnp.zeros((16, 128), f32)
            carry_b = jnp.zeros((16, 128), f32)
            for j in range(places):
                r = places - 1 - j
                carry_f = jnp.where(j < place, carry_f * hop + recv_ref[j, :, wide], carry_f)
                carry_b = jnp.where(r > place, carry_b * hop + recv_ref[r, :, wide], carry_b)
            for n in range(tiles):
                m = tiles - 1 - n
                st_ref[0, n] = carry_f
                st_ref[1, m] = carry_b
                carry_f = carry_f * jump
                carry_b = carry_b * jump
            conv = spread(local_ref[s, :, :, lanes], spread_f_ref, spread_b_ref, st_ref, lanes)
            z_ref[:, wide] = (sg[:, lanes] * conv.reshape(rows, 128)).astype(bf16)
    flip = reversal(chans)
    for n, ref in enumerate(outs):
        ref[...] = partial_chunk(n, copies, z_ref, w_buf, flip).astype(bf16)


def rest_kernel(chunks, z_ref, wo_ref, *refs):
    outs, (z_buf, w_buf, sems) = refs[:-3], refs[-3:]
    arrive = pltpu.make_async_copy(z_ref, z_buf, sems.at[len(chunks), 0])
    arrive.start()
    copies = fetch_columns(chunks, wo_ref, w_buf, sems)
    flip = reversal(w_buf.shape[2])
    arrive.wait()
    for n in range(len(chunks)):
        outs[n // 2][n % 2] = partial_chunk(n, copies, z_buf, w_buf, flip).astype(bf16)


def far_memory(*arrays):
    return [pltpu.with_memory_space_constraint(a, pltpu.HBM) for a in arrays]


def whole(shape):
    return pl.BlockSpec(shape, lambda *_: (0,) * len(shape))


remote = pl.BlockSpec(memory_space=pl.ANY)


def body(
    hidden, norm_gain, value_weight, gate_weight, value_taps, gate_taps, rates, residues, out_weight
):
    rows, chans = hidden.shape
    tp = lax.axis_size("tp")
    ring = tp // 2
    places = lax.axis_size("seq")
    modes = rates.shape[0]
    tiles = rows // T
    shape = pltpu.HBM
    params = pltpu.CompilerParams(vmem_limit_bytes=24 << 20)

    def turn(a, hop):
        return lax.ppermute(
            a, "tp", [(c * ring + i, c * ring + (i + hop) % ring) for c in range(2) for i in range(ring)]
        )

    def across(a):
        return lax.ppermute(a, "tp", [(i, (i + ring) % tp) for i in range(tp)])

    rates, residues = far_memory(rates, residues)
    powers, near, spread_f, spread_b = pl.pallas_call(
        tables_kernel,
        out_shape=(
            shape((T + 2, modes, chans), f32),
            shape((2 * T + 8, chans), f32),
            shape((modes, T, chans), f32),
            shape((modes, T, chans), f32),
        ),
        compiler_params=params,
        name="tables",
    )(rates, residues)
    gain = norm_gain.reshape(tp, 1, chans)
    value_weight, gate_weight, out_weight = far_memory(value_weight, gate_weight, out_weight)
    gain, value_taps, gate_taps = far_memory(gain, value_taps, gate_taps)

    def project(arrays, slots, carried):
        return pl.pallas_call(
            functools.partial(early_kernel, slots, len(arrays), len(carried)),
            in_specs=[remote] * len(arrays) + [whole(gain.shape), remote, remote] + [remote] * len(carried),
            out_specs=[remote, remote],
            out_shape=(shape((2, rows, 2 * chans), f32), shape((rows, 128), f32)),
            scratch_shapes=[
                pltpu.VMEM((2, rows, 2 * chans), f32),
                pltpu.VMEM((rows, 128), f32),
                pltpu.VMEM((len(slots), rows, chans), bf16),
                pltpu.VMEM((len(slots), 2, chans, 2 * chans), bf16),
                pltpu.SemaphoreType.DMA((len(slots) + 2, 5)),
            ],
            compiler_params=params,
            cost_estimate=pl.CostEstimate(
                flops=len(slots) * 10 * chans**3, transcendentals=0, bytes_accessed=len(slots) * 10 * chans**2
            ),
            name="project",
        )(*arrays, gain, value_weight, gate_weight, *carried)

    def pair_slots(hops):
        return tuple((n, c, c, hop) for n, hop in enumerate(hops) for c in range(2))

    start = jnp.stack([hidden, across(hidden)])
    up1, down1 = turn(start, 1), turn(start, -1)
    up1, powers, near, spread_f, spread_b = lax.optimization_barrier((up1, powers, near, spread_f, spread_b))
    up2, down2 = turn(up1, 1), turn(down1, -1)
    carried = project([start, up1, down1], pair_slots((0, -1, 1)), ())
    up2, carried = lax.optimization_barrier((up2, carried))
    up3, down3 = turn(up2, 1), turn(down2, -1)
    carried = project([up2, down2], pair_slots((-2, 2)), far_memory(*carried))
    up3, carried = lax.optimization_barrier((up3, carried))
    last_up, last_down = turn(up3[0], 1), turn(down3[1], -1)

    slots = pair_slots((-3, 3)) + ((2, None, 0, -4), (3, None, 1, 4))
    send, sv, gates, edge = pl.pallas_call(
        functools.partial(states_kernel, slots, 4),
        in_specs=[remote] * 4 + [whole(gain.shape), remote, remote, remote, remote]
        + [whole(value_taps.shape), whole(powers.shape)],
        out_specs=[
            whole((places, modes, 2 * chans + 128)),
            whole((2, tiles, T, chans)),
            whole((rows, 2 * chans)),
            whole((2, 2, 8, chans)),
        ],
        out_shape=(
            shape((places, modes, 2 * chans + 128), f32),
            shape((2, tiles, T, chans), f32),
            shape((rows, 2 * chans), f32),
            shape((2, 2, 8, chans), f32),
        ),
        scratch_shapes=[
            pltpu.VMEM((2, rows, 2 * chans), f32),
            pltpu.VMEM((rows, 128), f32),
            pltpu.VMEM((rows + 16, chans), f32),
            pltpu.VMEM((len(slots), rows, chans), bf16),
            pltpu.VMEM((len(slots), 2, chans, 2 * chans), bf16),
            pltpu.SemaphoreType.DMA((len(slots) + 1, 5)),
        ],
        compiler_params=params,
        name="states",
    )(
        up3, down3, last_up, last_down, gain, value_weight, gate_weight, *far_memory(*carried), value_taps,
        *far_memory(powers),
    )

    recv = lax.all_to_all(send, "seq", split_axis=0, concat_axis=0)
    local = pl.pallas_call(
        local_kernel,
        out_shape=shape((2, tiles, T, chans), f32),
        scratch_shapes=[pltpu.VMEM((2, tiles, modes, 128), f32)],
        compiler_params=params,
        name="local",
    )(*far_memory(sv, edge, powers, near, spread_f, spread_b))

    chunks = ((0, 4), (1, 4))
    square = shape((rows, chans), bf16)
    pair = shape((2, rows, chans), bf16)
    inputs = (
        recv, *far_memory(local, gates), gate_taps, rates,
        *far_memory(spread_f, spread_b),
    )
    z, out_up, out_down = pl.pallas_call(
        functools.partial(gated_kernel, chunks),
        in_specs=[whole(a.shape) for a in inputs] + [remote],
        out_specs=[whole((rows, 2 * chans)), whole((rows, chans)), whole((rows, chans))],
        out_shape=(shape((rows, 2 * chans), bf16), square, square),
        scratch_shapes=[
            pltpu.VMEM((rows + 16, chans), f32),
            pltpu.VMEM((2, tiles, modes, 128), f32),
            pltpu.VMEM((len(chunks), 2, chans, chans), bf16),
            pltpu.SemaphoreType.DMA((len(chunks), 2)),
        ],
        compiler_params=params,
        name="gated",
    )(*inputs, out_weight)

    def rest(z, hops):
        chunks = tuple((c, hop) for hop in hops for c in range(2))
        return pl.pallas_call(
            functools.partial(rest_kernel, chunks),
            in_specs=[remote, remote],
            out_specs=[whole((2, rows, chans))] * len(hops),
            out_shape=(pair,) * len(hops),
            scratch_shapes=[
                pltpu.VMEM(z.shape, bf16),
                pltpu.VMEM((len(chunks), 2, chans, chans), bf16),
                pltpu.SemaphoreType.DMA((len(chunks) + 1, 2)),
            ],
            compiler_params=params,
            cost_estimate=pl.CostEstimate(
                flops=len(chunks) * 6 * chans**3, transcendentals=0, bytes_accessed=len(chunks) * 6 * chans**2
            ),
            name="rest",
        )(*far_memory(z), out_weight)

    up_sum, down_sum = turn(out_up, 1), turn(out_down, -1)
    nothing = jnp.zeros_like(up_sum, f32)
    up_sum = jnp.stack([up_sum.astype(f32), nothing])
    down_sum = jnp.stack([nothing, down_sum.astype(f32)])
    parts = rest(z, (3, -3))
    for hop in (2, 1, 0):
        ups_now = (parts[0].astype(f32) + up_sum).astype(bf16)
        downs_now = (parts[1].astype(f32) + down_sum).astype(bf16)
        _, _, z = lax.optimization_barrier((ups_now, downs_now, z))
        up_sum, down_sum = turn(ups_now, 1).astype(f32), turn(downs_now, -1).astype(f32)
        parts = rest(z, (hop, -hop) if hop else (0,))
    total = parts[0].astype(f32) + up_sum + down_sum
    other = across(total[1].astype(bf16))
    return (total[0] + other.astype(f32)).astype(bf16)


def solution(mesh):
    in_specs = (
        P("seq", "tp"),
        P(),
        P(None, "tp"),
        P(None, "tp"),
        P(None, "tp"),
        P(None, "tp"),
        P(None, "tp"),
        P(None, "tp"),
        P("tp", None),
    )
    out_specs = P("seq", "tp")
    return jax.shard_map(body, mesh=mesh, in_specs=in_specs, out_specs=out_specs, check_vma=False)
```
